256 devices in a mesh: qa: 8 (over y, z_hi), qb: 32 (over x, z_lo, core).
Axes of the slice: x: 4, y: 4, z: 8 (z_hi: 2, z_lo: 4; z = z_hi * 4 + z_lo), core: 2. Of those that a mesh axis runs over, the one named last changes fastest.
Arguments:
- state: float32 [2, 8, 32, 65536], P(None, 'qa', 'qb'), may hold values from -6 to 6
- adjoint: float32 [2, 8, 32, 65536], P(None, 'qa', 'qb'), may hold values from -6 to 6
- gates: float32 [8, 2, 128, 128], replicated, may hold values from -1 to 1, as said below
Outputs:
- state_out: float32 [2, 8, 32, 65536], P(None, 'qa', 'qb')
- adjoint_out: float32 [2, 8, 32, 65536], P(None, 'qa', 'qb')
- gate_grads: float32 [8, 2, 128, 128], replicated
The draws below stay inside these ranges and needn't reach their ends.
Inputs may be any that keep to these rules, and one draw needn't show every extreme that they name: gates[k, 0] + i gates[k, 1] is a unitary 128 x 128 matrix for every k.
All inputs are finite; a program needn't handle non-finite values.
Results may differ from the reference program's by a relative error of at most 0.0001.
Values sent between devices are 32-bit elements; how exact they have to be, the bound alone decides.
A program may use at most 64 MiB of HBM per device.

```python
import math
import jax
import jax.numpy as jnp
from jax import lax

GATE_DIM = 128
AMP_DEV = 65536
GATES = 8
N_QA = 8
N_QB = 32


precise = lax.Precision.HIGHEST


def complex_dot(left_real, left_imag, right_real, right_imag):
    out_real = jnp.dot(left_real, right_real, precision=precise) - jnp.dot(left_imag, right_imag, precision=precise)
    out_imag = jnp.dot(left_real, right_imag, precision=precise) + jnp.dot(left_imag, right_real, precision=precise)
    return (out_real, out_imag)


def one_unitary(subkey):
    phases = jax.random.uniform(subkey, (3, GATE_DIM), jnp.float32, -math.pi, math.pi)
    indices = jnp.arange(GATE_DIM, dtype=jnp.int32)
    product = indices[:, None] * indices[None, :] % GATE_DIM
    angles = product.astype(jnp.float32) * (-2.0 * math.pi / GATE_DIM)
    norming = 1.0 / math.sqrt(GATE_DIM)
    dft_real = jnp.cos(angles) * norming
    dft_imag = jnp.sin(angles) * norming
    cosines = jnp.cos(phases)
    sines = jnp.sin(phases)
    mat_real = dft_real * cosines[2][None, :] - dft_imag * sines[2][None, :]
    mat_imag = dft_real * sines[2][None, :] + dft_imag * cosines[2][None, :]
    rot_real = cosines[1][:, None] * mat_real - sines[1][:, None] * mat_imag
    rot_imag = cosines[1][:, None] * mat_imag + sines[1][:, None] * mat_real
    mat_real, mat_imag = complex_dot(dft_real, dft_imag, rot_real, rot_imag)
    fin_real = cosines[0][:, None] * mat_real - sines[0][:, None] * mat_imag
    fin_imag = cosines[0][:, None] * mat_imag + sines[0][:, None] * mat_real
    return jnp.stack([fin_real, fin_imag])


def draw_gates(key, part):
    subkeys = jax.random.split(jax.random.fold_in(key, 17), GATES)
    return jax.vmap(one_unitary)(subkeys).astype(jnp.float32)


def level_of(rng, shape, shards, low, top_value):
    gain, own = 1.0, jax.random.fold_in(rng, 6)
    for position, shards_of in shards:
        draws = jnp.exp(jax.random.uniform(jax.random.fold_in(own, position), (shards_of,), jnp.float32, low / len(shards), top_value / len(shards)))
        gain = gain * jnp.repeat(draws, shape[position] // shards_of).reshape([-1 if axis == position else 1 for axis in range(len(shape))])
    return gain


def noise(rng, extent, width, reach, pieces=(), kind=jnp.bfloat16):
    gain = level_of(rng, extent, pieces, -0.22, 0.18) if pieces else 1.0
    result = jax.random.normal(rng, extent, jnp.float32) * width * gain
    return jnp.minimum(jnp.maximum(result, -reach), reach).astype(kind)


def setup_inputs(seed: int = 0) -> dict:
    splits = jax.random.split(jax.random.key(seed), 4)
    state = noise(splits[0], (2, N_QA, N_QB, AMP_DEV), 1.0, 6.0, ((1, 8), (2, 32)), jnp.float32)
    adjoint = noise(splits[1], (2, N_QA, N_QB, AMP_DEV), 1.0, 6.0, ((1, 8), (2, 32)), jnp.float32)
    gates = draw_gates(jax.random.fold_in(splits[3], 71), 0)
    return dict(state=state, adjoint=adjoint, gates=gates)


precise = lax.Precision.HIGHEST


def undo_high(real_part, imag_part, gate_real, gate_imag):
    shape = real_part.shape
    gate_size = gate_real.shape[0]
    folded = (shape[0] * shape[1], gate_size, shape[2] // gate_size)
    fold_real = real_part.reshape(folded)
    fold_imag = imag_part.reshape(folded)

    def mixing(matrix, field):
        return jnp.einsum('hg,phm->pgm', matrix, field, precision=precise)

    new_real = mixing(gate_real, fold_real) + mixing(gate_imag, fold_imag)
    new_imag = mixing(gate_real, fold_imag) - mixing(gate_imag, fold_real)
    return new_real.reshape(shape), new_imag.reshape(shape)


def undo_low(real_part, imag_part, gate_real, gate_imag):
    shape = real_part.shape
    gate_size = gate_real.shape[0]
    fold_real = real_part.reshape(-1, gate_size)
    fold_imag = imag_part.reshape(-1, gate_size)

    def mixing(field, matrix):
        return jnp.einsum('rh,hg->rg', field, matrix, precision=precise)

    new_real = mixing(fold_real, gate_real) + mixing(fold_imag, gate_imag)
    new_imag = mixing(fold_imag, gate_real) - mixing(fold_real, gate_imag)
    return new_real.reshape(shape), new_imag.reshape(shape)


def pair_high(adjoint_real, adjoint_imag, new_real, new_imag, gate_size):
    shape = adjoint_real.shape
    folded = (shape[0] * shape[1], gate_size, shape[2] // gate_size)

    def inner(left, right):
        return jnp.einsum('pgm,phm->gh', left.reshape(folded), right.reshape(folded), precision=precise)

    grad_real = inner(adjoint_real, new_real) + inner(adjoint_imag, new_imag)
    grad_imag = inner(adjoint_imag, new_real) - inner(adjoint_real, new_imag)
    return jnp.stack([grad_real, grad_imag])


def pair_low(adjoint_real, adjoint_imag, new_real, new_imag, gate_size):
    def inner(left, right):
        return jnp.einsum('rg,rh->gh', left.reshape(-1, gate_size), right.reshape(-1, gate_size), precision=precise)

    grad_real = inner(adjoint_real, new_real) + inner(adjoint_imag, new_imag)
    grad_imag = inner(adjoint_imag, new_real) - inner(adjoint_real, new_imag)
    return jnp.stack([grad_real, grad_imag])


def swap_first(field):
    shape = field.shape
    return field.reshape(shape[0], shape[1], shape[0], shape[2] // shape[0]).transpose(2, 1, 0, 3).reshape(shape)


def swap_second(field):
    shape = field.shape
    return field.reshape(shape[0], shape[1], shape[1], shape[2] // shape[1]).transpose(0, 2, 1, 3).reshape(shape)


def reference(state, adjoint, gates):
    state_real, state_imag = state[0], state[1]
    adjoint_real, adjoint_imag = adjoint[0], adjoint[1]
    gate_size = gates.shape[-1]
    scaling = float(N_QA * N_QB * AMP_DEV // GATE_DIM) ** -0.5
    collected = []
    for index in range(GATES):
        gate_real = gates[index, 0]
        gate_imag = gates[index, 1]
        if index % 2 == 0:
            new_real, new_imag = undo_high(state_real, state_imag, gate_real, gate_imag)
            collected.append(scaling * pair_high(adjoint_real, adjoint_imag, new_real, new_imag, gate_size))
            adjoint_real, adjoint_imag = undo_high(adjoint_real, adjoint_imag, gate_real, gate_imag)
        else:
            new_real, new_imag = undo_low(state_real, state_imag, gate_real, gate_imag)
            collected.append(scaling * pair_low(adjoint_real, adjoint_imag, new_real, new_imag, gate_size))
            adjoint_real, adjoint_imag = undo_low(adjoint_real, adjoint_imag, gate_real, gate_imag)
        state_real, state_imag = new_real, new_imag
        if index % 2 == 1:
            if (index // 2) % 2 == 0:
                permute = swap_first
            else:
                permute = swap_second
            state_real = permute(state_real)
            state_imag = permute(state_imag)
            adjoint_real = permute(adjoint_real)
            adjoint_imag = permute(adjoint_imag)
    state_out = jnp.stack([state_real, state_imag])
    adjoint_out = jnp.stack([adjoint_real, adjoint_imag])
    return state_out, adjoint_out, jnp.stack(collected)
```

```python
import functools

import jax
import jax.numpy as jnp
from jax import lax
from jax.experimental import pallas as pl
from jax.experimental.pallas import tpu as pltpu
from jax.sharding import PartitionSpec as P

F32 = jnp.float32
BF16 = jnp.bfloat16
MESH = pl.DeviceIdType.MESH
N_QA, N_QB, N_DEV = 8, 32, 256
ROWS = N_DEV * 8
GROWS = 5 * 256


def split(x):
    hi = x.astype(BF16)
    return hi, (x - hi.astype(F32)).astype(BF16)


def dot3(a, b, ca, cb):
    ah, al = split(a)
    bh, bl = split(b)
    left = jnp.concatenate([ah, al, ah], axis=ca)
    right = jnp.concatenate([bh, bh, bl], axis=cb)
    return lax.dot_general(left, right, (((ca,), (cb,)), ((), ())), preferred_element_type=F32)


def conj_embed(re, im):
    return jnp.concatenate(
        [jnp.concatenate([re, -im], axis=1), jnp.concatenate([im, re], axis=1)], axis=0
    )


def swap_bits(vs, shift):
    vs = list(vs)
    lane = lax.broadcasted_iota(jnp.int32, vs[0].shape, 1)
    bit = 0
    while (1 << bit) < len(vs):
        stride = 1 << (shift + bit)
        upper = (lane & stride) != 0
        for i in range(len(vs)):
            if i & (1 << bit):
                continue
            k = i | (1 << bit)
            lo, hi = vs[i], vs[k]
            vs[i] = jnp.where(upper, pltpu.roll(hi, stride, 1), lo)
            vs[k] = jnp.where(upper, hi, pltpu.roll(lo, 128 - stride, 1))
        bit += 1
    return vs


def swap_outer(ref):
    def body(b, _):
        at = [pl.ds(pl.multiple_of((a * 32 + b) * 8, 8), 8) for a in range(8)]
        for s, v in zip(at, swap_bits([ref[s, :] for s in at], 4)):
            ref[s, :] = v
        return 0

    lax.fori_loop(0, 32, body, 0, unroll=2)


def swap_inner(ref):
    def body(a, _):
        at = [pl.ds(pl.multiple_of((a * 32 + b) * 8, 8), 8) for b in range(32)]
        for s, v in zip(at, swap_bits([ref[s, :] for s in at], 2)):
            ref[s, :] = v
        return 0

    lax.fori_loop(0, 8, body, 0)


def quadrants(q):
    return q[:128, :128] + q[128:, 128:], q[128:, :128] - q[:128, 128:]


def low_kernel(state_ref, adjoint_ref, gates_ref, y_ref, rho_ref):
    fields = []
    for ref in (state_ref, adjoint_ref):
        fields.append(jnp.concatenate([ref[0], ref[1]], axis=1))
    rho_re, rho_im = quadrants(dot3(fields[1], fields[0], 0, 0))
    rho_ref[0:128, :] = rho_re
    rho_ref[128:256, :] = rho_im
    top = jnp.concatenate([gates_ref[1, 0], -gates_ref[1, 1]], axis=1)
    for k in (3, 5, 7):
        top = dot3(top, conj_embed(gates_ref[k, 0], gates_ref[k, 1]), 1, 0)
    joined = conj_embed(top[:, :128], -top[:, 128:])
    for m in range(4):
        rows = []
        for ref in (state_ref, adjoint_ref):
            rows.append(
                jnp.concatenate([ref[r, pl.ds(m, 128, stride=4), :] for r in range(2)], axis=1)
            )
        out = dot3(joined, jnp.concatenate(rows, axis=0), 0, 1)
        for r in range(2):
            for f in range(2):
                j = r * 4 + f * 2 + m // 2
                y_ref[pl.ds((m % 2) * 1024 + j, 128, stride=8), :] = out[
                    r * 128 : (r + 1) * 128, f * 128 : (f + 1) * 128
                ]


def high_kernel(z_ref, gates_ref, w_ref, grad_ref):
    w_ref[...] = z_ref[...]

    def gate(index, slot):
        embedded = conj_embed(gates_ref[index, 0], gates_ref[index, 1])
        old = []
        for f in range(2):
            old.append(
                jnp.concatenate(
                    [
                        jnp.concatenate(
                            [w_ref[pl.ds(r * 4 + f * 2 + m, 256, stride=8), :] for r in range(2)],
                            axis=1,
                        )
                        for m in range(2)
                    ],
                    axis=0,
                )
            )
        new = [dot3(x, embedded, 1, 0) for x in old]
        grad_re, grad_im = quadrants(dot3(old[1], new[0], 0, 0))
        grad_ref[pl.ds(slot * 256, 128), :] = grad_re
        grad_ref[pl.ds(slot * 256 + 128, 128), :] = grad_im
        for f in range(2):
            for m in range(2):
                for r in range(2):
                    w_ref[pl.ds(r * 4 + f * 2 + m, 256, stride=8), :] = new[f][
                        m * 256 : (m + 1) * 256, r * 128 : (r + 1) * 128
                    ]

    gate(0, 0)
    swap_outer(w_ref)
    gate(2, 1)
    swap_inner(w_ref)
    gate(4, 2)
    swap_outer(w_ref)
    gate(6, 3)
    swap_inner(w_ref)


def greet_all():
    qa, qb = lax.axis_index("qa"), lax.axis_index("qb")
    barrier = pltpu.get_barrier_semaphore()

    def greet(i, _):
        there = (lax.rem(qa + i // 32, 8), lax.rem(qb + lax.rem(i, 32), 32))
        pl.semaphore_signal(barrier, inc=1, device_id=there, device_id_type=MESH)
        return 0

    lax.fori_loop(1, N_DEV, greet, 0)
    pl.semaphore_wait(barrier, N_DEV - 1)


def tile(index):
    return pl.ds(pl.multiple_of(index * 8, 8), 8)


def send_all(src_ref, dst_ref, send_sem, recv_sem):
    qa, qb = lax.axis_index("qa"), lax.axis_index("qb")
    me = qa * N_QB + qb

    def send(i, _):
        a, b = lax.rem(qa + i // 32, 8), lax.rem(qb + lax.rem(i, 32), 32)
        pltpu.make_async_remote_copy(
            src_ref=src_ref.at[tile(a * N_QB + b)],
            dst_ref=dst_ref.at[tile(me)],
            send_sem=send_sem,
            recv_sem=recv_sem,
            device_id=(a, b),
            device_id_type=MESH,
        ).start()
        return 0

    lax.fori_loop(1, N_DEV, send, 0)
    dst_ref[tile(me), :] = src_ref[tile(me), :]


def await_rows(ref, rows, send_sem, recv_sem):
    qa, qb = lax.axis_index("qa"), lax.axis_index("qb")
    pltpu.make_async_remote_copy(
        src_ref=ref.at[pl.ds(0, rows)],
        dst_ref=ref.at[pl.ds(0, rows)],
        send_sem=send_sem,
        recv_sem=recv_sem,
        device_id=(qa, qb),
        device_id_type=MESH,
    ).wait()


def exchange_kernel(x_ref, o_ref, send_sem, recv_sem):
    greet_all()
    send_all(x_ref, o_ref, send_sem, recv_sem)
    await_rows(o_ref, ROWS - 8, send_sem, recv_sem)


def place():
    qa, qb = lax.axis_index("qa"), lax.axis_index("qb")
    return qb // 8, qa // 2, lax.rem(qa, 2) * 4 + lax.rem(qb // 2, 4), lax.rem(qb, 2)


def device(x, y, z, c):
    return (y * 2 + z // 4, x * 8 + lax.rem(z, 4) * 2 + c)


def rows_at(start, size):
    return pl.ds(pl.multiple_of(start, 8), size)


def reduce_all(part_ref, sum_ref, half_ref, quarter_ref, eighth_ref, columns_ref, acc_refs, send, recv):
    x, y, z, c = place()
    acc0, acc1, acc2 = acc_refs

    def put(stage, src, dst, there):
        pltpu.make_async_remote_copy(
            src_ref=src, dst_ref=dst, send_sem=send.at[stage], recv_sem=recv.at[stage],
            device_id=there, device_id_type=MESH,
        ).start()

    put(0, part_ref.at[rows_at((1 - c) * 640, 640)], half_ref, device(x, y, z, 1 - c))
    await_rows(half_ref, 640, send.at[0], recv.at[0])
    acc0[...] = part_ref[rows_at(c * 640, 640), :] + half_ref[...]
    for d in range(1, 4):
        to = lax.rem(x + d, 4)
        put(1, acc0.at[rows_at(to * 160, 160)], quarter_ref.at[pl.ds((d - 1) * 160, 160)], device(to, y, z, c))
    await_rows(quarter_ref, 480, send.at[1], recv.at[1])
    acc1[...] = (
        acc0[rows_at(x * 160, 160), :]
        + quarter_ref[0:160, :]
        + quarter_ref[160:320, :]
        + quarter_ref[320:480, :]
    )
    for d in range(1, 4):
        to = lax.rem(y + d, 4)
        put(2, acc1.at[rows_at(to * 40, 40)], eighth_ref.at[pl.ds((d - 1) * 40, 40)], device(x, to, z, c))
    await_rows(eighth_ref, 120, send.at[2], recv.at[2])
    acc2[...] = (
        acc1[rows_at(y * 40, 40), :] + eighth_ref[0:40, :] + eighth_ref[40:80, :] + eighth_ref[80:120, :]
    )
    for d in range(1, 8):
        put(3, acc2, columns_ref.at[rows_at(z * 40, 40)], device(x, y, lax.rem(z + d, 8), c))
    columns_ref[rows_at(z * 40, 40), :] = acc2[...]
    await_rows(columns_ref, 280, send.at[3], recv.at[3])
    total = columns_ref[0:40, :]
    for k in range(1, 8):
        total = total + columns_ref[k * 40 : (k + 1) * 40, :]
    mine = rows_at(c * 640 + x * 160 + y * 40, 40)
    sum_ref[mine, :] = total
    for d in range(1, 4):
        put(4, sum_ref.at[mine], sum_ref.at[mine], device(x, lax.rem(y + d, 4), z, c))
    await_rows(sum_ref, 120, send.at[4], recv.at[4])
    mine = rows_at(c * 640 + x * 160, 160)
    for d in range(1, 4):
        put(5, sum_ref.at[mine], sum_ref.at[mine], device(lax.rem(x + d, 4), y, z, c))
    await_rows(sum_ref, 480, send.at[5], recv.at[5])
    mine = rows_at(c * 640, 640)
    put(6, sum_ref.at[mine], sum_ref.at[mine], device(x, y, z, 1 - c))
    await_rows(sum_ref, 640, send.at[6], recv.at[6])


def last_exchange_kernel(
    x_ref, part_ref, o_ref, sum_ref, half_ref, quarter_ref, eighth_ref, columns_ref,
    acc0, acc1, acc2, send_sem, recv_sem, send, recv,
):
    greet_all()
    send_all(x_ref, o_ref, send_sem, recv_sem)
    reduce_all(
        part_ref, sum_ref, half_ref, quarter_ref, eighth_ref, columns_ref, (acc0, acc1, acc2), send, recv
    )
    await_rows(o_ref, ROWS - 8, send_sem, recv_sem)


def finish_kernel(scaling, r_ref, sum_ref, gates_ref, state_ref, adjoint_ref, grads_ref):
    for f, ref in enumerate((state_ref, adjoint_ref)):
        for r in range(2):
            for m in range(4):
                j = r * 4 + f * 2 + m // 2
                block = r_ref[pl.ds((m % 2) * 1024 + j, 128, stride=8), :]
                ref[r, pl.ds(m, 128, stride=4), :] = block.T
    for slot in range(4):
        for r in range(2):
            grads_ref[2 * slot, r] = scaling * sum_ref[pl.ds(slot * 256 + r * 128, 128), :]
    rho = scaling * jnp.concatenate(
        [sum_ref[pl.ds(1024, 128), :], sum_ref[pl.ds(1152, 128), :]], axis=1
    )
    for k in (1, 3, 5, 7):
        re, im = gates_ref[k, 0], gates_ref[k, 1]
        grad = dot3(rho, conj_embed(re, -im), 1, 0)
        grad_re, grad_im = grad[:, :128], grad[:, 128:]
        grads_ref[k, 0] = grad_re
        grads_ref[k, 1] = grad_im
        if k < 7:
            right = jnp.concatenate(
                [jnp.concatenate([grad_re, grad_im], axis=1), jnp.concatenate([grad_im, -grad_re], axis=1)],
                axis=0,
            )
            rho = dot3(jnp.concatenate([re, im], axis=0), right, 0, 0)


VMEM = pl.BlockSpec(memory_space=pltpu.VMEM)


def local_call(kernel, outs, *args):
    return pl.pallas_call(
        kernel,
        out_shape=[jax.ShapeDtypeStruct(s, F32) for s in outs],
        in_specs=[VMEM] * len(args),
        out_specs=[VMEM] * len(outs),
        compiler_params=pltpu.CompilerParams(vmem_limit_bytes=48 << 20),
    )(*args)


def shards(state, adjoint, gates):
    scaling = float(N_DEV * 65536 // 128) ** -0.5
    y, rho = local_call(
        low_kernel, [(ROWS, 128), (256, 128)], state.reshape(2, 512, 128), adjoint.reshape(2, 512, 128), gates
    )
    z = pl.pallas_call(
        exchange_kernel,
        out_shape=jax.ShapeDtypeStruct((ROWS, 128), F32),
        in_specs=[VMEM],
        out_specs=VMEM,
        scratch_shapes=[pltpu.SemaphoreType.DMA, pltpu.SemaphoreType.DMA],
        compiler_params=pltpu.CompilerParams(collective_id=0, has_side_effects=True),
    )(y)
    w, grads = local_call(high_kernel, [(ROWS, 128), (1024, 128)], z, gates)
    parts = jnp.concatenate([grads, rho], axis=0)
    r, sums = pl.pallas_call(
        last_exchange_kernel,
        out_shape=[jax.ShapeDtypeStruct((ROWS, 128), F32), jax.ShapeDtypeStruct((GROWS, 128), F32)],
        in_specs=[VMEM] * 2,
        out_specs=[VMEM] * 2,
        scratch_shapes=[
            pltpu.VMEM((640, 128), F32),
            pltpu.VMEM((480, 128), F32),
            pltpu.VMEM((120, 128), F32),
            pltpu.VMEM((320, 128), F32),
            pltpu.VMEM((640, 128), F32),
            pltpu.VMEM((160, 128), F32),
            pltpu.VMEM((40, 128), F32),
            pltpu.SemaphoreType.DMA,
            pltpu.SemaphoreType.DMA,
            pltpu.SemaphoreType.DMA((7,)),
            pltpu.SemaphoreType.DMA((7,)),
        ],
        compiler_params=pltpu.CompilerParams(collective_id=1, has_side_effects=True),
    )(w, parts)
    state_out, adjoint_out, grads_out = local_call(
        functools.partial(finish_kernel, scaling), [(2, 512, 128), (2, 512, 128), (8, 2, 128, 128)], r, sums, gates
    )
    return state_out.reshape(state.shape), adjoint_out.reshape(adjoint.shape), grads_out


def solution(mesh):
    in_specs = (P(None, "qa", "qb", None), P(None, "qa", "qb", None), P())
    out_specs = (P(None, "qa", "qb", None), P(None, "qa", "qb", None), P())
    return jax.shard_map(shards, mesh=mesh, in_specs=in_specs, out_specs=out_specs, check_vma=False)
```

```python
import functools

import jax
import jax.numpy as jnp
from jax import lax
from jax.experimental import pallas as pl
from jax.experimental.pallas import tpu as pltpu
from jax.sharding import PartitionSpec as P

F32 = jnp.float32
BF16 = jnp.bfloat16
MESH = pl.DeviceIdType.MESH
N_QA, N_QB, N_DEV = 8, 32, 256
ROWS = N_DEV * 8
GROWS = 5 * 256


def split(x):
    hi = x.astype(BF16)
    return hi, (x - hi.astype(F32)).astype(BF16)


def dot3(a, b, ca, cb):
    ah, al = split(a)
    bh, bl = split(b)
    left = jnp.concatenate([ah, al, ah], axis=ca)
    right = jnp.concatenate([bh, bh, bl], axis=cb)
    return lax.dot_general(left, right, (((ca,), (cb,)), ((), ())), preferred_element_type=F32)


def conj_embed(re, im):
    return jnp.concatenate(
        [jnp.concatenate([re, -im], axis=1), jnp.concatenate([im, re], axis=1)], axis=0
    )


def undo_matrix(gates_ref, k):
    re, im = gates_ref[k, 0].T, gates_ref[k, 1].T
    hi, lo = split(
        jnp.concatenate(
            [jnp.concatenate([re, im], axis=1), jnp.concatenate([-im, re], axis=1)], axis=0
        )
    )
    return jnp.concatenate([hi, lo, hi], axis=1)


def undo(matrix, x):
    hi, lo = split(x)
    return jnp.dot(matrix, jnp.concatenate([hi, hi, lo], axis=0), preferred_element_type=F32)


def quadrants(q):
    return q[:128, :128] + q[128:, 128:], q[128:, :128] - q[:128, 128:]


def cat(parts, axis):
    return jnp.concatenate(list(parts), axis=axis)


def store_gradient(part_ref, slot, q):
    re, im = quadrants(q)
    part_ref[pl.ds(slot * 256, 128), :] = re
    part_ref[pl.ds(slot * 256 + 128, 128), :] = im


def before_kernel(fields, gates_ref, x_ref, y_ref, part_ref):
    matrix = undo_matrix(gates_ref, 0)
    old = [
        cat((cat((ref[r, pl.ds(m, 128, stride=4), :] for m in range(4)), 1) for r in range(2)), 0)
        for ref in fields
    ]
    new = [undo(matrix, x) for x in old]
    for f in range(2):
        for r in range(2):
            for m in range(4):
                x_ref[pl.ds(((f * 2 + r) * 4 + m) * 128, 128), :] = new[f][
                    r * 128 : (r + 1) * 128, m * 128 : (m + 1) * 128
                ]
    store_gradient(part_ref, 0, dot3(old[1], new[0], 1, 1))
    flat = [cat((ref[0], ref[1]), 1) for ref in fields]
    store_gradient(part_ref, 4, dot3(flat[1], flat[0], 0, 0))
    top = cat((gates_ref[1, 0], -gates_ref[1, 1]), 1)
    for k in (3, 5, 7):
        top = dot3(top, conj_embed(gates_ref[k, 0], gates_ref[k, 1]), 1, 0)
    joined = cat((top[:, :128].T, top[:, 128:].T), 1)
    for m0 in range(2):
        straight, crossed = [], []
        for t in range(8):
            for f in range(2):
                for m1 in range(2):
                    re, im = (
                        x_ref[pl.ds(((f * 2 + r) * 4 + m1 * 2 + m0) * 128 + t * 16, 16), :]
                        for r in range(2)
                    )
                    straight += [re, im]
                    crossed += [-im, re]
        out = dot3(joined, cat((cat(straight, 0), cat(crossed, 0)), 1), 1, 1)
        for t in range(8):
            y_ref[pl.ds(m0 * 1024 + (t % 2) * 4 + t // 2, 128, stride=8), :] = out[
                :, t * 128 : (t + 1) * 128
            ]


def block1(t0, m1, f):
    return ((t0 * 2 + m1) * 2 + f) * 256


FOUR = [(t0, m1) for t0 in range(2) for m1 in range(2)]


def load1(ref, f):
    return cat((ref[pl.ds(block1(t0, m1, f), 256), :] for t0, m1 in FOUR), 1)


def load2(ref, t):
    return cat((ref[pl.ds(t * 256 + r, 128, stride=2), :] for r in range(2)), 0)


def load3(ref, b1):
    return cat(
        (ref[pl.ds(t * 256 + b1 * 32 + r, 16, stride=2), :] for r in range(2) for t in range(8)), 0
    )


def between_kernel(z_ref, one_ref, one_new_ref, two_ref, two_new_ref, w_ref, matrices):
    for a in range(8):
        for t0 in range(2):
            rows = cat((z_ref[pl.ds(a * 256 + t0 * 4 + t, 32, stride=8), :] for t in range(4)), 0).T
            for f in range(2):
                for m1 in range(2):
                    for r in range(2):
                        at = ((f * 2 + m1) * 2 + r) * 16
                        one_ref[pl.ds(block1(t0, m1, f) + r * 128 + a * 16, 16), :] = rows[at : at + 16]
    for f in range(2):
        new = undo(matrices[0], load1(one_ref, f))
        for i, (t0, m1) in enumerate(FOUR):
            one_new_ref[pl.ds(block1(t0, m1, f), 256), :] = new[:, i * 128 : (i + 1) * 128]
    for t0 in range(2):
        for v in range(4):
            for r in range(2):
                rows = cat(
                    (
                        one_new_ref[pl.ds(block1(t0, m1, f) + r * 128 + v, 32, stride=4), :]
                        for f in range(2)
                        for m1 in range(2)
                    ),
                    0,
                ).T
                for t in range(4):
                    two_ref[pl.ds((t * 2 + t0) * 256 + v * 2 + r, 32, stride=8), :] = rows[
                        t * 32 : (t + 1) * 32
                    ]
    for half in range(2):
        new = undo(matrices[1], cat((load2(two_ref, half * 4 + i) for i in range(4)), 1))
        for i in range(4):
            for r in range(2):
                two_new_ref[pl.ds((half * 4 + i) * 256 + r, 128, stride=2), :] = new[
                    r * 128 : (r + 1) * 128, i * 128 : (i + 1) * 128
                ]
    for half in range(2):
        new = undo(matrices[2], cat((load3(two_new_ref, half * 4 + i) for i in range(4)), 1))
        for i in range(4):
            for r in range(2):
                w_ref[pl.ds((half * 4 + i) * 256 + r, 128, stride=2), :] = new[
                    r * 128 : (r + 1) * 128, i * 128 : (i + 1) * 128
                ]


def lane_gradient(old, new):
    upper = lax.broadcasted_iota(jnp.int32, (256, 128), 1) >= 64
    total = None
    for i in range(0, 8, 2):
        left = jnp.where(upper, old[i](), pltpu.roll(old[i + 1](), 64, 1))
        right = jnp.where(upper, pltpu.roll(new[i](), 64, 1), new[i + 1]())
        q = dot3(left, right, 1, 1)
        total = q if total is None else total + q
    return total


def gradients(part_ref, one_ref, one_new_ref, two_ref, two_new_ref, w_ref):
    store_gradient(part_ref, 1, dot3(load1(one_ref, 1), load1(one_new_ref, 0), 1, 1))
    each = range(8)
    store_gradient(
        part_ref,
        2,
        lane_gradient(
            [functools.partial(load2, two_ref, t) for t in each],
            [functools.partial(load2, two_new_ref, t) for t in each],
        ),
    )
    store_gradient(
        part_ref,
        3,
        lane_gradient(
            [functools.partial(load3, two_new_ref, b) for b in each],
            [functools.partial(load2, w_ref, b) for b in each],
        ),
    )


def greet_all():
    qa, qb = lax.axis_index("qa"), lax.axis_index("qb")
    barrier = pltpu.get_barrier_semaphore()

    def greet(i, _):
        there = (lax.rem(qa + i // 32, 8), lax.rem(qb + lax.rem(i, 32), 32))
        pl.semaphore_signal(barrier, inc=1, device_id=there, device_id_type=MESH)
        return 0

    lax.fori_loop(1, N_DEV, greet, 0)


def await_all():
    pl.semaphore_wait(pltpu.get_barrier_semaphore(), N_DEV - 1)


def tile(index):
    return pl.ds(pl.multiple_of(index * 8, 8), 8)


def send_all(src_ref, dst_ref, send_sem, recv_sem):
    qa, qb = lax.axis_index("qa"), lax.axis_index("qb")
    me = qa * N_QB + qb

    def send(i, _):
        a, b = lax.rem(qa + i // 32, 8), lax.rem(qb + lax.rem(i, 32), 32)
        pltpu.make_async_remote_copy(
            src_ref=src_ref.at[tile(a * N_QB + b)],
            dst_ref=dst_ref.at[tile(me)],
            send_sem=send_sem,
            recv_sem=recv_sem,
            device_id=(a, b),
            device_id_type=MESH,
        ).start()
        return 0

    lax.fori_loop(1, N_DEV, send, 0)
    dst_ref[tile(me), :] = src_ref[tile(me), :]


def await_rows(ref, rows, send_sem, recv_sem):
    qa, qb = lax.axis_index("qa"), lax.axis_index("qb")
    pltpu.make_async_remote_copy(
        src_ref=ref.at[pl.ds(0, rows)],
        dst_ref=ref.at[pl.ds(0, rows)],
        send_sem=send_sem,
        recv_sem=recv_sem,
        device_id=(qa, qb),
        device_id_type=MESH,
    ).wait()


def place():
    qa, qb = lax.axis_index("qa"), lax.axis_index("qb")
    return qb // 8, qa // 2, lax.rem(qa, 2) * 4 + lax.rem(qb // 2, 4), lax.rem(qb, 2)


def device(x, y, z, c):
    return (y * 2 + z // 4, x * 8 + lax.rem(z, 4) * 2 + c)


def rows_at(start, size):
    return pl.ds(pl.multiple_of(start, 8), size)


def reduce_all(part_ref, sum_ref, half_ref, quarter_ref, eighth_ref, columns_ref, acc_refs, send, recv):
    x, y, z, c = place()
    acc0, acc1, acc2 = acc_refs

    def put(stage, src, dst, there):
        pltpu.make_async_remote_copy(
            src_ref=src, dst_ref=dst, send_sem=send.at[stage], recv_sem=recv.at[stage],
            device_id=there, device_id_type=MESH,
        ).start()

    put(0, part_ref.at[rows_at((1 - c) * 640, 640)], half_ref, device(x, y, z, 1 - c))
    await_rows(half_ref, 640, send.at[0], recv.at[0])
    acc0[...] = part_ref[rows_at(c * 640, 640), :] + half_ref[...]
    for d in range(1, 4):
        to = lax.rem(x + d, 4)
        put(1, acc0.at[rows_at(to * 160, 160)], quarter_ref.at[pl.ds((d - 1) * 160, 160)], device(to, y, z, c))
    await_rows(quarter_ref, 480, send.at[1], recv.at[1])
    acc1[...] = (
        acc0[rows_at(x * 160, 160), :]
        + quarter_ref[0:160, :]
        + quarter_ref[160:320, :]
        + quarter_ref[320:480, :]
    )
    for d in range(1, 4):
        to = lax.rem(y + d, 4)
        put(2, acc1.at[rows_at(to * 40, 40)], eighth_ref.at[pl.ds((d - 1) * 40, 40)], device(x, to, z, c))
    await_rows(eighth_ref, 120, send.at[2], recv.at[2])
    acc2[...] = (
        acc1[rows_at(y * 40, 40), :] + eighth_ref[0:40, :] + eighth_ref[40:80, :] + eighth_ref[80:120, :]
    )
    for d in range(1, 8):
        put(3, acc2, columns_ref.at[rows_at(z * 40, 40)], device(x, y, lax.rem(z + d, 8), c))
    columns_ref[rows_at(z * 40, 40), :] = acc2[...]
    await_rows(columns_ref, 280, send.at[3], recv.at[3])
    total = columns_ref[0:40, :]
    for k in range(1, 8):
        total = total + columns_ref[k * 40 : (k + 1) * 40, :]
    mine = rows_at(c * 640 + x * 160 + y * 40, 40)
    sum_ref[mine, :] = total
    for d in range(1, 4):
        put(4, sum_ref.at[mine], sum_ref.at[mine], device(x, lax.rem(y + d, 4), z, c))
    await_rows(sum_ref, 120, send.at[4], recv.at[4])
    mine = rows_at(c * 640 + x * 160, 160)
    for d in range(1, 4):
        put(5, sum_ref.at[mine], sum_ref.at[mine], device(lax.rem(x + d, 4), y, z, c))
    await_rows(sum_ref, 480, send.at[5], recv.at[5])
    mine = rows_at(c * 640, 640)
    put(6, sum_ref.at[mine], sum_ref.at[mine], device(x, y, z, 1 - c))
    await_rows(sum_ref, 640, send.at[6], recv.at[6])


def main_kernel(
    state_ref, adjoint_ref, gates_ref, r_ref, sum_ref,
    x_ref, y_ref, z_ref, one_ref, one_new_ref, two_ref, two_new_ref, w_ref, part_ref,
    half_ref, quarter_ref, eighth_ref, columns_ref, acc0, acc1, acc2,
    sends, recvs, send, recv,
):
    greet_all()
    before_kernel((state_ref, adjoint_ref), gates_ref, x_ref, y_ref, part_ref)
    await_all()
    send_all(y_ref, z_ref, sends.at[0], recvs.at[0])
    matrices = [undo_matrix(gates_ref, k) for k in (2, 4, 6)]
    await_rows(z_ref, ROWS - 8, sends.at[0], recvs.at[0])
    between_kernel(z_ref, one_ref, one_new_ref, two_ref, two_new_ref, w_ref, matrices)
    send_all(w_ref, r_ref, sends.at[1], recvs.at[1])
    gradients(part_ref, one_ref, one_new_ref, two_ref, two_new_ref, w_ref)
    reduce_all(
        part_ref, sum_ref, half_ref, quarter_ref, eighth_ref, columns_ref, (acc0, acc1, acc2), send, recv
    )
    await_rows(r_ref, ROWS - 8, sends.at[1], recvs.at[1])


def finish_kernel(scaling, r_ref, sum_ref, gates_ref, state_ref, adjoint_ref, grads_ref):
    for m0 in range(2):
        for v in range(4):
            for r in range(2):
                rows = r_ref[pl.ds(m0 * 1024 + v * 2 + r, 128, stride=8), :].T
                for f, ref in enumerate((state_ref, adjoint_ref)):
                    for m1 in range(2):
                        at = (f * 2 + m1) * 32
                        ref[r, pl.ds(v * 4 + m1 * 2 + m0, 32, stride=16), :] = rows[at : at + 32]
    for slot in range(4):
        for r in range(2):
            grads_ref[2 * slot, r] = scaling * sum_ref[pl.ds(slot * 256 + r * 128, 128), :]
    rho = scaling * jnp.concatenate(
        [sum_ref[pl.ds(1024, 128), :], sum_ref[pl.ds(1152, 128), :]], axis=1
    )
    for k in (1, 3, 5, 7):
        re, im = gates_ref[k, 0], gates_ref[k, 1]
        grad = dot3(rho, conj_embed(re, -im), 1, 0)
        grad_re, grad_im = grad[:, :128], grad[:, 128:]
        grads_ref[k, 0] = grad_re
        grads_ref[k, 1] = grad_im
        if k < 7:
            right = jnp.concatenate(
                [jnp.concatenate([grad_re, grad_im], axis=1), jnp.concatenate([grad_im, -grad_re], axis=1)],
                axis=0,
            )
            rho = dot3(jnp.concatenate([re, im], axis=0), right, 0, 0)


VMEM = pl.BlockSpec(memory_space=pltpu.VMEM)


def local_call(kernel, outs, *args):
    return pl.pallas_call(
        kernel,
        out_shape=[jax.ShapeDtypeStruct(s, F32) for s in outs],
        in_specs=[VMEM] * len(args),
        out_specs=[VMEM] * len(outs),
        compiler_params=pltpu.CompilerParams(vmem_limit_bytes=48 << 20),
    )(*args)


def shards(state, adjoint, gates):
    scaling = float(N_DEV * 65536 // 128) ** -0.5
    buffer = pltpu.VMEM((ROWS, 128), F32)
    r, sums = pl.pallas_call(
        main_kernel,
        out_shape=[jax.ShapeDtypeStruct((ROWS, 128), F32), jax.ShapeDtypeStruct((GROWS, 128), F32)],
        in_specs=[VMEM] * 3,
        out_specs=[VMEM] * 2,
        scratch_shapes=[
            *[buffer] * 8,
            pltpu.VMEM((GROWS, 128), F32),
            pltpu.VMEM((640, 128), F32),
            pltpu.VMEM((480, 128), F32),
            pltpu.VMEM((120, 128), F32),
            pltpu.VMEM((320, 128), F32),
            pltpu.VMEM((640, 128), F32),
            pltpu.VMEM((160, 128), F32),
            pltpu.VMEM((40, 128), F32),
            pltpu.SemaphoreType.DMA((2,)),
            pltpu.SemaphoreType.DMA((2,)),
            pltpu.SemaphoreType.DMA((7,)),
            pltpu.SemaphoreType.DMA((7,)),
        ],
        compiler_params=pltpu.CompilerParams(
            collective_id=0, has_side_effects=True, vmem_limit_bytes=40 << 20
        ),
    )(state.reshape(2, 512, 128), adjoint.reshape(2, 512, 128), gates)
    state_out, adjoint_out, grads_out = local_call(
        functools.partial(finish_kernel, scaling), [(2, 512, 128), (2, 512, 128), (8, 2, 128, 128)], r, sums, gates
    )
    return state_out.reshape(state.shape), adjoint_out.reshape(adjoint.shape), grads_out


def solution(mesh):
    in_specs = (P(None, "qa", "qb", None), P(None, "qa", "qb", None), P())
    out_specs = (P(None, "qa", "qb", None), P(None, "qa", "qb", None), P())
    return jax.shard_map(shards, mesh=mesh, in_specs=in_specs, out_specs=out_specs, check_vma=False)
```

```python
import functools

import jax
import jax.numpy as jnp
from jax import lax
from jax.experimental import pallas as pl
from jax.experimental.pallas import tpu as pltpu
from jax.sharding import PartitionSpec as P

F32 = jnp.float32
BF16 = jnp.bfloat16
MESH = pl.DeviceIdType.MESH
N_QA, N_QB, N_DEV = 8, 32, 256
HALF = N_DEV * 4
GROWS = 5 * 256


def split(x):
    hi = x.astype(BF16)
    return hi, (x - hi.astype(F32)).astype(BF16)


def dot3(a, b, ca, cb):
    ah, al = split(a)
    bh, bl = split(b)
    left = jnp.concatenate([ah, al, ah], axis=ca)
    right = jnp.concatenate([bh, bh, bl], axis=cb)
    return lax.dot_general(left, right, (((ca,), (cb,)), ((), ())), preferred_element_type=F32)


def conj_embed(re, im):
    return jnp.concatenate(
        [jnp.concatenate([re, -im], axis=1), jnp.concatenate([im, re], axis=1)], axis=0
    )


def undo_matrix(gates_ref, k):
    re, im = gates_ref[k, 0].T, gates_ref[k, 1].T
    hi, lo = split(
        jnp.concatenate(
            [jnp.concatenate([re, im], axis=1), jnp.concatenate([-im, re], axis=1)], axis=0
        )
    )
    return jnp.concatenate([hi, lo, hi], axis=1)


def undo_lanes_matrix(gates_ref, k):
    hi, lo = split(jnp.concatenate([gates_ref[k, 0].T, gates_ref[k, 1].T], axis=1))
    return jnp.concatenate([hi, lo, hi], axis=1)


def undo(matrix, x):
    hi, lo = split(x)
    return jnp.dot(matrix, jnp.concatenate([hi, hi, lo], axis=0), preferred_element_type=F32)


def quadrants(q):
    return q[:128, :128] + q[128:, 128:], q[128:, :128] - q[:128, 128:]


def cat(parts, axis):
    return jnp.concatenate(list(parts), axis=axis)


def store_gradient(part_ref, slot, re, im):
    part_ref[pl.ds(slot * 256, 128), :] = re
    part_ref[pl.ds(slot * 256 + 128, 128), :] = im


def before_kernel(fields, gates_ref, x_ref, y_refs, part_ref):
    matrix = undo_matrix(gates_ref, 0)
    old = [
        cat((cat((ref[r, pl.ds(m, 128, stride=4), :] for m in range(4)), 1) for r in range(2)), 0)
        for ref in fields
    ]
    new = [undo(matrix, x) for x in old]
    for f in range(2):
        for r in range(2):
            for m in range(4):
                x_ref[pl.ds(((f * 2 + r) * 4 + m) * 128, 128), :] = new[f][
                    r * 128 : (r + 1) * 128, m * 128 : (m + 1) * 128
                ]
    store_gradient(part_ref, 0, *quadrants(dot3(old[1], new[0], 1, 1)))
    flat = [cat((ref[0], ref[1]), 1) for ref in fields]
    store_gradient(part_ref, 1, *quadrants(dot3(flat[1], flat[0], 0, 0)))
    top = cat((gates_ref[1, 0], -gates_ref[1, 1]), 1)
    for k in (3, 5, 7):
        top = dot3(top, conj_embed(gates_ref[k, 0], gates_ref[k, 1]), 1, 0)
    joined = cat((top[:, :128].T, top[:, 128:].T), 1)
    for m1 in range(2):
        for m0 in range(2):
            straight, crossed = [], []
            for t21 in range(4):
                for f in range(2):
                    for t0 in range(2):
                        re, im = (
                            x_ref[
                                pl.ds(((f * 2 + r) * 4 + m1 * 2 + m0) * 128 + (t21 * 2 + t0) * 16, 16), :
                            ]
                            for r in range(2)
                        )
                        straight += [re, im]
                        crossed += [-im, re]
            out = dot3(joined, cat((cat(straight, 0), cat(crossed, 0)), 1), 1, 1)
            for t21 in range(4):
                y_refs[m1][pl.ds(m0 * 512 + t21, 128, stride=4), :] = out[:, t21 * 128 : (t21 + 1) * 128]


def turned(x):
    upper = lax.broadcasted_iota(jnp.int32, x.shape, 1) >= 64
    rolled = pltpu.roll(x, 64, 1)
    return jnp.where(upper, -rolled, rolled)


def load1(ref, f):
    return cat((ref[pl.ds((t0 * 2 + f) * 256, 256), :] for t0 in range(2)), 1)


def load2(ref, t):
    return ref[pl.ds(t * 128, 128), :]


def load3(ref, b1):
    return cat((ref[pl.ds(t * 128 + b1 * 16, 16), :] for t in range(8)), 0)


def undo_lanes(matrix, load):
    blocks = [load(i) for i in range(8)]
    return undo(matrix, cat((cat(blocks, 1), cat((turned(x) for x in blocks), 1)), 0))


def between_kernel(z_ref, one_ref, one_new_ref, two_ref, two_new_ref, w_ref, matrices, after=lambda k: None):
    for a in range(8):
        rows = cat((z_ref[pl.ds(a * 128 + t, 32, stride=4), :] for t in range(4)), 0).T
        for f in range(2):
            for t0 in range(2):
                for r in range(2):
                    at = ((f * 2 + t0) * 2 + r) * 16
                    one_ref[pl.ds((t0 * 2 + f) * 256 + r * 128 + a * 16, 16), :] = rows[at : at + 16]
    new = undo(matrices[0], cat((load1(one_ref, f) for f in range(2)), 1))
    for f in range(2):
        for t0 in range(2):
            one_new_ref[pl.ds((t0 * 2 + f) * 256, 256), :] = new[
                :, (f * 2 + t0) * 128 : (f * 2 + t0 + 1) * 128
            ]
    after(0)
    for t0 in range(2):
        for v in range(4):
            rows = cat(
                (
                    one_new_ref[pl.ds((t0 * 2 + f) * 256 + r * 128 + v, 32, stride=4), :]
                    for r in range(2)
                    for f in range(2)
                ),
                0,
            ).T
            for t in range(4):
                two_ref[pl.ds((t * 2 + t0) * 128 + v, 32, stride=4), :] = rows[t * 32 : (t + 1) * 32]
    new = undo_lanes(matrices[1], functools.partial(load2, two_ref))
    for t in range(8):
        two_new_ref[pl.ds(t * 128, 128), :] = new[:, t * 128 : (t + 1) * 128]
    after(1)
    new = undo_lanes(matrices[2], functools.partial(load3, two_new_ref))
    for b1 in range(8):
        w_ref[pl.ds(b1 * 128, 128), :] = new[:, b1 * 128 : (b1 + 1) * 128]
    after(2)


def lane_gradient(load_old, old_ref, load_new, new_ref):
    lane = lax.broadcasted_iota(jnp.int32, (128, 128), 1)
    adjoint = (lane & 32) != 0
    lefts, rights, crosses = [], [], []
    for i in range(0, 8, 2):
        lefts.append(
            jnp.where(adjoint, load_old(old_ref, i), pltpu.roll(load_old(old_ref, i + 1), 96, 1))
        )
        right = jnp.where(adjoint, pltpu.roll(load_new(new_ref, i), 32, 1), load_new(new_ref, i + 1))
        rights.append(right)
        crosses.append(-turned(right))
    q = dot3(cat(lefts, 1), cat((cat(rights, 1), cat(crosses, 1)), 0), 1, 1)
    return q[:, :128], q[:, 128:]


def gradient(k, one_ref, one_new_ref, two_ref, two_new_ref, w_ref):
    if k == 0:
        return quadrants(dot3(load1(one_ref, 1), load1(one_new_ref, 0), 1, 1))
    if k == 1:
        return lane_gradient(load2, two_ref, load2, two_new_ref)
    return lane_gradient(load3, two_new_ref, load2, w_ref)


def low_gradients(scaling, sum_ref, gates_ref, low_ref):
    rho = scaling * cat((sum_ref[pl.ds(256, 128), :], sum_ref[pl.ds(384, 128), :]), 1)
    for i, k in enumerate((1, 3, 5, 7)):
        re, im = gates_ref[k, 0], gates_ref[k, 1]
        grad = dot3(rho, conj_embed(re, -im), 1, 0)
        grad_re, grad_im = grad[:, :128], grad[:, 128:]
        low_ref[i, 0] = grad_re
        low_ref[i, 1] = grad_im
        if k < 7:
            right = cat((cat((grad_re, grad_im), 1), cat((grad_im, -grad_re), 1)), 0)
            rho = dot3(cat((re, im), 0), right, 0, 0)


def greet_all():
    qa, qb = lax.axis_index("qa"), lax.axis_index("qb")
    barrier = pltpu.get_barrier_semaphore()

    def greet(i, _):
        there = (lax.rem(qa + i // 32, 8), lax.rem(qb + lax.rem(i, 32), 32))
        pl.semaphore_signal(barrier, inc=1, device_id=there, device_id_type=MESH)
        return 0

    lax.fori_loop(1, N_DEV, greet, 0)


def await_all():
    pl.semaphore_wait(pltpu.get_barrier_semaphore(), N_DEV - 1)


def tile(index):
    return pl.ds(pl.multiple_of(index * 4, 4), 4)


def send_blocks(src_ref, dst_ref, send_sem, recv_sem, first=0, last=N_DEV):
    qa, qb = lax.axis_index("qa"), lax.axis_index("qb")
    me = qa * N_QB + qb

    def send(i, _):
        a, b = lax.rem(qa + i // 32, 8), lax.rem(qb + lax.rem(i, 32), 32)
        pltpu.make_async_remote_copy(
            src_ref=src_ref.at[tile(a * N_QB + b)],
            dst_ref=dst_ref.at[tile(me)],
            send_sem=send_sem,
            recv_sem=recv_sem,
            device_id=(a, b),
            device_id_type=MESH,
        ).start()
        return 0

    lax.fori_loop(max(first, 1), last, send, 0)
    if first == 0:
        dst_ref[tile(me), :] = src_ref[tile(me), :]


def await_rows(ref, rows, send_sem, recv_sem):
    qa, qb = lax.axis_index("qa"), lax.axis_index("qb")
    pltpu.make_async_remote_copy(
        src_ref=ref.at[pl.ds(0, rows)],
        dst_ref=ref.at[pl.ds(0, rows)],
        send_sem=send_sem,
        recv_sem=recv_sem,
        device_id=(qa, qb),
        device_id_type=MESH,
    ).wait()


def place():
    qa, qb = lax.axis_index("qa"), lax.axis_index("qb")
    return qb // 8, qa // 2, lax.rem(qa, 2) * 4 + lax.rem(qb // 2, 4), lax.rem(qb, 2)


def device(x, y, z, c):
    return (y * 2 + z // 4, x * 8 + lax.rem(z, 4) * 2 + c)


def rows_at(start, size):
    return pl.ds(pl.multiple_of(start, 8), size)


class GradientSum:
    def __init__(self, part_ref, sum_ref, slots, refs, send, recv):
        self.part, self.sum, self.slots = part_ref, sum_ref, slots
        self.got, self.mine, self.columns = refs
        self.send, self.recv = send, recv
        self.x, self.y, self.z, self.c = place()
        self.piece = self.y * 8 + self.x * 2 + self.c

    def put(self, stage, src, dst, there):
        pltpu.make_async_remote_copy(
            src_ref=src, dst_ref=dst, send_sem=self.send.at[stage], recv_sem=self.recv.at[stage],
            device_id=device(*there), device_id_type=MESH,
        ).start()

    def plane(self, body):
        def step(d, _):
            other = lax.rem(self.piece + d, 32)
            body(d, other, (lax.rem(other // 2, 4), other // 8, self.z, lax.rem(other, 2)))
            return 0

        lax.fori_loop(1, 32, step, 0)

    def rows(self, slot, piece):
        return rows_at(slot * 256 + piece * 8, 8)

    def start_slot(self, i):
        def body(d, other, there):
            self.put(i, self.part.at[self.rows(self.slots[i], other)], self.got.at[rows_at((i * 32 + d) * 8, 8)], there)

        self.plane(body)

    def start_columns(self):
        n = len(self.slots)
        for i, slot in enumerate(self.slots):
            await_rows(self.got, 31 * 8, self.send.at[i], self.recv.at[i])
            total = self.part[self.rows(slot, self.piece), :]
            for d in range(1, 32):
                total = total + self.got[(i * 32 + d) * 8 : (i * 32 + d + 1) * 8, :]
            self.mine[i * 8 : (i + 1) * 8, :] = total
        here = rows_at(self.z * n * 8, n * 8)
        for d in range(1, 8):
            self.put(n, self.mine, self.columns.at[here], (self.x, self.y, lax.rem(self.z + d, 8), self.c))
        self.columns[here, :] = self.mine[...]

    def start_plane(self):
        n = len(self.slots)
        await_rows(self.columns, 7 * n * 8, self.send.at[n], self.recv.at[n])
        for i, slot in enumerate(self.slots):
            total = self.columns[i * 8 : (i + 1) * 8, :]
            for k in range(1, 8):
                total = total + self.columns[(k * n + i) * 8 : (k * n + i + 1) * 8, :]
            self.sum[self.rows(slot, self.piece), :] = total

        def body(d, other, there):
            for slot in self.slots:
                mine = self.sum.at[self.rows(slot, self.piece)]
                self.put(n + 1, mine, mine, there)

        self.plane(body)

    def finish(self):
        n = len(self.slots)
        await_rows(self.sum, 31 * n * 8, self.send.at[n + 1], self.recv.at[n + 1])


def sum_scratch(slots):
    return [pltpu.VMEM((n * slots, 128), F32) for n in (256, 8, 64)]


def main_kernel(
    scaling,     state_hbm, adjoint_hbm, gates_hbm, r0_ref, r1_ref, sum_ref, low_ref,
    state_ref, adjoint_ref, gates_ref, x_ref,
    y0, y1, z0, z1, w0, w1, one0, one1, one_new0, one_new1, two0, two1, two_new0, two_new1, part_ref,
    a1, a2, a3, b1, b2, b3,
    loads, sends, recvs, send_a, recv_a, send_b, recv_b,
):
    pairs = ((state_hbm, state_ref), (adjoint_hbm, adjoint_ref), (gates_hbm, gates_ref))
    copies = [pltpu.make_async_copy(src, dst, loads.at[i]) for i, (src, dst) in enumerate(pairs)]
    for copy in copies:
        copy.start()
    greet_all()
    for copy in copies:
        copy.wait()
    before_kernel((state_ref, adjoint_ref), gates_ref, x_ref, (y0, y1), part_ref)
    early = GradientSum(part_ref, sum_ref, (0, 1), (a1, a2, a3), send_a, recv_a)
    late = GradientSum(part_ref, sum_ref, (2, 3, 4), (b1, b2, b3), send_b, recv_b)
    one = (one0, one_new0, two0, two_new0, w0)
    two = (one1, one_new1, two1, two_new1, w1)
    await_all()
    early.start_slot(0)
    early.start_slot(1)
    send_blocks(y0, z0, sends.at[0], recvs.at[0])
    send_blocks(y1, z1, sends.at[1], recvs.at[1])
    matrices = [undo_matrix(gates_ref, 2)] + [undo_lanes_matrix(gates_ref, k) for k in (4, 6)]
    early.start_columns()
    await_rows(z0, HALF - 4, sends.at[0], recvs.at[0])
    between_kernel(z0, *one, matrices)
    send_blocks(w0, r0_ref, sends.at[2], recvs.at[2])
    first = [gradient(k, *one) for k in range(3)]
    early.start_plane()
    await_rows(z1, HALF - 4, sends.at[1], recvs.at[1])

    def after(k):
        (re0, im0), (re1, im1) = first[k], gradient(k, *two)
        store_gradient(part_ref, 2 + k, re0 + re1, im0 + im1)
        late.start_slot(k)

    between_kernel(z1, *two, matrices, after)
    send_blocks(w1, r1_ref, sends.at[3], recvs.at[3], 0, 128)
    late.start_columns()
    send_blocks(w1, r1_ref, sends.at[3], recvs.at[3], 128, N_DEV)
    early.finish()
    low_gradients(scaling, sum_ref, gates_ref, low_ref)
    late.start_plane()
    late.finish()
    for i, r_ref in enumerate((r0_ref, r1_ref)):
        await_rows(r_ref, HALF - 4, sends.at[2 + i], recvs.at[2 + i])


def finish_kernel(scaling, r0_ref, r1_ref, sum_ref, low_ref, state_ref, adjoint_ref, grads_ref):
    for m1, from_ref in enumerate((r0_ref, r1_ref)):
        for m0 in range(2):
            for v in range(4):
                rows = from_ref[pl.ds(m0 * 512 + v, 128, stride=4), :].T
                for r in range(2):
                    for f, ref in enumerate((state_ref, adjoint_ref)):
                        at = (r * 2 + f) * 32
                        ref[r, pl.ds(v * 4 + m1 * 2 + m0, 32, stride=16), :] = rows[at : at + 32]
    for k, slot in ((0, 0), (2, 2), (4, 3), (6, 4)):
        for r in range(2):
            grads_ref[k, r] = scaling * sum_ref[pl.ds(slot * 256 + r * 128, 128), :]
    for i in range(4):
        grads_ref[2 * i + 1] = low_ref[i]


VMEM = pl.BlockSpec(memory_space=pltpu.VMEM)


def local_call(kernel, outs, *args):
    return pl.pallas_call(
        kernel,
        out_shape=[jax.ShapeDtypeStruct(s, F32) for s in outs],
        in_specs=[VMEM] * len(args),
        out_specs=[VMEM] * len(outs),
        compiler_params=pltpu.CompilerParams(vmem_limit_bytes=48 << 20),
    )(*args)


def shards(state, adjoint, gates):
    scaling = float(N_DEV * 65536 // 128) ** -0.5
    half = pltpu.VMEM((HALF, 128), F32)
    hbm = pl.BlockSpec(memory_space=pltpu.HBM)
    received = jax.ShapeDtypeStruct((HALF, 128), F32)
    r0, r1, sums, low = pl.pallas_call(
        functools.partial(main_kernel, scaling),
        out_shape=[
            received,
            received,
            jax.ShapeDtypeStruct((GROWS, 128), F32),
            jax.ShapeDtypeStruct((4, 2, 128, 128), F32),
        ],
        in_specs=[hbm] * 3,
        out_specs=[VMEM] * 4,
        scratch_shapes=[
            pltpu.VMEM((2, 512, 128), F32),
            pltpu.VMEM((2, 512, 128), F32),
            pltpu.VMEM((8, 2, 128, 128), F32),
            pltpu.VMEM((2048, 128), F32),
            *[half] * 14,
            pltpu.VMEM((GROWS, 128), F32),
            *sum_scratch(2),
            *sum_scratch(3),
            pltpu.SemaphoreType.DMA((3,)),
            pltpu.SemaphoreType.DMA((4,)),
            pltpu.SemaphoreType.DMA((4,)),
            *[pltpu.SemaphoreType.DMA((5,))] * 4,
        ],
        compiler_params=pltpu.CompilerParams(
            collective_id=0, has_side_effects=True, vmem_limit_bytes=40 << 20
        ),
    )(state.reshape(2, 512, 128), adjoint.reshape(2, 512, 128), gates)
    state_out, adjoint_out, grads_out = local_call(
        functools.partial(finish_kernel, scaling),
        [(2, 512, 128), (2, 512, 128), (8, 2, 128, 128)],
        r0, r1, sums, low,
    )
    return state_out.reshape(state.shape), adjoint_out.reshape(adjoint.shape), grads_out


def solution(mesh):
    in_specs = (P(None, "qa", "qb", None), P(None, "qa", "qb", None), P())
    out_specs = (P(None, "qa", "qb", None), P(None, "qa", "qb", None), P())
    return jax.shard_map(shards, mesh=mesh, in_specs=in_specs, out_specs=out_specs, check_vma=False)
```

```python
import functools

import jax
import jax.numpy as jnp
from jax import lax
from jax.experimental import pallas as pl
from jax.experimental.pallas import tpu as pltpu
from jax.sharding import PartitionSpec as P

F32 = jnp.float32
BF16 = jnp.bfloat16
MESH = pl.DeviceIdType.MESH
N_QA, N_QB, N_DEV = 8, 32, 256
HALF = N_DEV * 4
GROWS = 5 * 256


def split(x):
    hi = x.astype(BF16)
    return hi, (x - hi.astype(F32)).astype(BF16)


def dot3(a, b, ca, cb):
    ah, al = split(a)
    bh, bl = split(b)
    left = jnp.concatenate([ah, al, ah], axis=ca)
    right = jnp.concatenate([bh, bh, bl], axis=cb)
    return lax.dot_general(left, right, (((ca,), (cb,)), ((), ())), preferred_element_type=F32)


def conj_embed(re, im):
    return jnp.concatenate(
        [jnp.concatenate([re, -im], axis=1), jnp.concatenate([im, re], axis=1)], axis=0
    )


def undo_matrix(gates_ref, k):
    re, im = gates_ref[k, 0].T, gates_ref[k, 1].T
    hi, lo = split(
        jnp.concatenate(
            [jnp.concatenate([re, im], axis=1), jnp.concatenate([-im, re], axis=1)], axis=0
        )
    )
    return jnp.concatenate([hi, lo, hi], axis=1)


def undo_lanes_matrix(gates_ref, k):
    hi, lo = split(jnp.concatenate([gates_ref[k, 0].T, gates_ref[k, 1].T], axis=1))
    return jnp.concatenate([hi, lo, hi], axis=1)


def undo(matrix, x):
    hi, lo = split(x)
    return jnp.dot(matrix, jnp.concatenate([hi, hi, lo], axis=0), preferred_element_type=F32)


def quadrants(q):
    return q[:128, :128] + q[128:, 128:], q[128:, :128] - q[:128, 128:]


def cat(parts, axis):
    return jnp.concatenate(list(parts), axis=axis)


def store_gradient(part_ref, slot, re, im):
    part_ref[pl.ds(slot * 256, 128), :] = re
    part_ref[pl.ds(slot * 256 + 128, 128), :] = im


def undo_first(fields, gates_ref, x_ref):
    matrix = undo_matrix(gates_ref, 0)
    for f, ref in enumerate(fields):
        old = cat(
            (cat((ref[r, pl.ds(m, 128, stride=4), :] for m in range(4)), 1) for r in range(2)), 0
        )
        new = undo(matrix, old)
        for r in range(2):
            for m in range(4):
                x_ref[pl.ds(((f * 2 + r) * 4 + m) * 128, 128), :] = new[
                    r * 128 : (r + 1) * 128, m * 128 : (m + 1) * 128
                ]


def join_low(gates_ref):
    top = cat((gates_ref[1, 0], -gates_ref[1, 1]), 1)
    for k in (3, 5, 7):
        top = dot3(top, conj_embed(gates_ref[k, 0], gates_ref[k, 1]), 1, 0)
    return cat((top[:, :128].T, top[:, 128:].T), 1)


def undo_low(joined, m1, x_ref, y_ref):
    for m0 in range(2):
        straight, crossed = [], []
        for t21 in range(4):
            for f in range(2):
                for t0 in range(2):
                    re, im = (
                        x_ref[pl.ds(((f * 2 + r) * 4 + m1 * 2 + m0) * 128 + (t21 * 2 + t0) * 16, 16), :]
                        for r in range(2)
                    )
                    straight += [re, im]
                    crossed += [-im, re]
        out = dot3(joined, cat((cat(straight, 0), cat(crossed, 0)), 1), 1, 1)
        for t21 in range(4):
            y_ref[pl.ds(m0 * 512 + t21, 128, stride=4), :] = out[:, t21 * 128 : (t21 + 1) * 128]


def first_gradients(fields, x_ref, part_ref):
    old = cat(
        (cat((fields[1][r, pl.ds(m, 128, stride=4), :] for m in range(4)), 1) for r in range(2)), 0
    )
    new = cat((cat((x_ref[pl.ds((r * 4 + m) * 128, 128), :] for m in range(4)), 1) for r in range(2)), 0)
    store_gradient(part_ref, 0, *quadrants(dot3(old, new, 1, 1)))
    flat = [cat((ref[0], ref[1]), 1) for ref in fields]
    store_gradient(part_ref, 1, *quadrants(dot3(flat[1], flat[0], 0, 0)))


def turned(x):
    upper = lax.broadcasted_iota(jnp.int32, x.shape, 1) >= 64
    rolled = pltpu.roll(x, 64, 1)
    return jnp.where(upper, -rolled, rolled)


def load1(ref, f):
    return cat((ref[pl.ds((t0 * 2 + f) * 256, 256), :] for t0 in range(2)), 1)


def load2(ref, t):
    return ref[pl.ds(t * 128, 128), :]


def load3(ref, b1):
    return cat((ref[pl.ds(t * 128 + b1 * 16, 16), :] for t in range(8)), 0)


def undo_lanes(matrix, load):
    blocks = [load(i) for i in range(8)]
    return undo(matrix, cat((cat(blocks, 1), cat((turned(x) for x in blocks), 1)), 0))


def between_kernel(z_ref, one_ref, one_new_ref, two_ref, two_new_ref, w_ref, matrices, after=lambda k: None):
    for a in range(8):
        rows = cat((z_ref[pl.ds(a * 128 + t, 32, stride=4), :] for t in range(4)), 0).T
        for f in range(2):
            for t0 in range(2):
                for r in range(2):
                    at = ((f * 2 + t0) * 2 + r) * 16
                    one_ref[pl.ds((t0 * 2 + f) * 256 + r * 128 + a * 16, 16), :] = rows[at : at + 16]
    new = undo(matrices[0], cat((load1(one_ref, f) for f in range(2)), 1))
    for f in range(2):
        for t0 in range(2):
            one_new_ref[pl.ds((t0 * 2 + f) * 256, 256), :] = new[
                :, (f * 2 + t0) * 128 : (f * 2 + t0 + 1) * 128
            ]
    after(0)
    for t0 in range(2):
        for v in range(4):
            rows = cat(
                (
                    one_new_ref[pl.ds((t0 * 2 + f) * 256 + r * 128 + v, 32, stride=4), :]
                    for r in range(2)
                    for f in range(2)
                ),
                0,
            ).T
            for t in range(4):
                two_ref[pl.ds((t * 2 + t0) * 128 + v, 32, stride=4), :] = rows[t * 32 : (t + 1) * 32]
    new = undo_lanes(matrices[1], functools.partial(load2, two_ref))
    for t in range(8):
        two_new_ref[pl.ds(t * 128, 128), :] = new[:, t * 128 : (t + 1) * 128]
    after(1)
    new = undo_lanes(matrices[2], functools.partial(load3, two_new_ref))
    for b1 in range(8):
        w_ref[pl.ds(b1 * 128, 128), :] = new[:, b1 * 128 : (b1 + 1) * 128]
    after(2)


def lane_gradient(load_old, old_ref, load_new, new_ref):
    lane = lax.broadcasted_iota(jnp.int32, (128, 128), 1)
    adjoint = (lane & 32) != 0
    lefts, rights, crosses = [], [], []
    for i in range(0, 8, 2):
        lefts.append(
            jnp.where(adjoint, load_old(old_ref, i), pltpu.roll(load_old(old_ref, i + 1), 96, 1))
        )
        right = jnp.where(adjoint, pltpu.roll(load_new(new_ref, i), 32, 1), load_new(new_ref, i + 1))
        rights.append(right)
        crosses.append(-turned(right))
    q = dot3(cat(lefts, 1), cat((cat(rights, 1), cat(crosses, 1)), 0), 1, 1)
    return q[:, :128], q[:, 128:]


def gradient(k, one_ref, one_new_ref, two_ref, two_new_ref, w_ref):
    if k == 0:
        return quadrants(dot3(load1(one_ref, 1), load1(one_new_ref, 0), 1, 1))
    if k == 1:
        return lane_gradient(load2, two_ref, load2, two_new_ref)
    return lane_gradient(load3, two_new_ref, load2, w_ref)


def low_gradients(scaling, sum_ref, gates_ref, low_ref):
    rho = scaling * cat((sum_ref[pl.ds(256, 128), :], sum_ref[pl.ds(384, 128), :]), 1)
    for i, k in enumerate((1, 3, 5, 7)):
        re, im = gates_ref[k, 0], gates_ref[k, 1]
        grad = dot3(rho, conj_embed(re, -im), 1, 0)
        grad_re, grad_im = grad[:, :128], grad[:, 128:]
        low_ref[i, 0] = grad_re
        low_ref[i, 1] = grad_im
        if k < 7:
            right = cat((cat((grad_re, grad_im), 1), cat((grad_im, -grad_re), 1)), 0)
            rho = dot3(cat((re, im), 0), right, 0, 0)


def greet_all():
    qa, qb = lax.axis_index("qa"), lax.axis_index("qb")
    barrier = pltpu.get_barrier_semaphore()

    def greet(i, _):
        there = (lax.rem(qa + i // 32 + 4, 8), lax.rem(qb + lax.rem(i, 32) + 16, 32))
        pl.semaphore_signal(barrier, inc=1, device_id=there, device_id_type=MESH)
        return 0

    lax.fori_loop(0, 144, greet, 0)
    lax.fori_loop(145, N_DEV, greet, 0)


def await_all():
    pl.semaphore_wait(pltpu.get_barrier_semaphore(), N_DEV - 1)


def tile(index):
    return pl.ds(pl.multiple_of(index * 4, 4), 4)


def send_blocks(src_ref, dst_ref, send_sem, recv_sem, first=0, last=N_DEV):
    qa, qb = lax.axis_index("qa"), lax.axis_index("qb")
    me = qa * N_QB + qb

    def send(i, _):
        a, b = lax.rem(qa + i // 32, 8), lax.rem(qb + lax.rem(i, 32), 32)
        pltpu.make_async_remote_copy(
            src_ref=src_ref.at[tile(a * N_QB + b)],
            dst_ref=dst_ref.at[tile(me)],
            send_sem=send_sem,
            recv_sem=recv_sem,
            device_id=(a, b),
            device_id_type=MESH,
        ).start()
        return 0

    lax.fori_loop(max(first, 1), last, send, 0)
    if first == 0:
        dst_ref[tile(me), :] = src_ref[tile(me), :]


def await_rows(ref, rows, send_sem, recv_sem):
    qa, qb = lax.axis_index("qa"), lax.axis_index("qb")
    pltpu.make_async_remote_copy(
        src_ref=ref.at[pl.ds(0, rows)],
        dst_ref=ref.at[pl.ds(0, rows)],
        send_sem=send_sem,
        recv_sem=recv_sem,
        device_id=(qa, qb),
        device_id_type=MESH,
    ).wait()


def place():
    qa, qb = lax.axis_index("qa"), lax.axis_index("qb")
    return qb // 8, qa // 2, lax.rem(qa, 2) * 4 + lax.rem(qb // 2, 4), lax.rem(qb, 2)


def device(x, y, z, c):
    return (y * 2 + z // 4, x * 8 + lax.rem(z, 4) * 2 + c)


def rows_at(start, size):
    return pl.ds(pl.multiple_of(start, 8), size)


class GradientSum:
    def __init__(self, part_ref, sum_ref, slots, refs, send, recv):
        self.part, self.sum, self.slots = part_ref, sum_ref, slots
        self.got, self.mine, self.columns = refs
        self.send, self.recv = send, recv
        self.x, self.y, self.z, self.c = place()
        self.piece = self.y * 8 + self.x * 2 + self.c

    def put(self, stage, src, dst, there):
        pltpu.make_async_remote_copy(
            src_ref=src, dst_ref=dst, send_sem=self.send.at[stage], recv_sem=self.recv.at[stage],
            device_id=device(*there), device_id_type=MESH,
        ).start()

    def plane(self, body):
        def step(d, _):
            other = lax.rem(self.piece + d, 32)
            body(d, other, (lax.rem(other // 2, 4), other // 8, self.z, lax.rem(other, 2)))
            return 0

        lax.fori_loop(1, 32, step, 0)

    def rows(self, slot, piece):
        return rows_at(slot * 256 + piece * 8, 8)

    def start_slot(self, i):
        def body(d, other, there):
            self.put(i, self.part.at[self.rows(self.slots[i], other)], self.got.at[rows_at((i * 32 + d) * 8, 8)], there)

        self.plane(body)

    def start_columns(self):
        n = len(self.slots)
        for i, slot in enumerate(self.slots):
            await_rows(self.got, 31 * 8, self.send.at[i], self.recv.at[i])
            total = self.part[self.rows(slot, self.piece), :]
            for d in range(1, 32):
                total = total + self.got[(i * 32 + d) * 8 : (i * 32 + d + 1) * 8, :]
            self.mine[i * 8 : (i + 1) * 8, :] = total
        here = rows_at(self.z * n * 8, n * 8)
        for d in range(1, 8):
            self.put(n, self.mine, self.columns.at[here], (self.x, self.y, lax.rem(self.z + d, 8), self.c))
        self.columns[here, :] = self.mine[...]

    def start_plane(self):
        n = len(self.slots)
        await_rows(self.columns, 7 * n * 8, self.send.at[n], self.recv.at[n])
        for i, slot in enumerate(self.slots):
            total = self.columns[i * 8 : (i + 1) * 8, :]
            for k in range(1, 8):
                total = total + self.columns[(k * n + i) * 8 : (k * n + i + 1) * 8, :]
            self.sum[self.rows(slot, self.piece), :] = total

        def body(d, other, there):
            for slot in self.slots:
                mine = self.sum.at[self.rows(slot, self.piece)]
                self.put(n + 1, mine, mine, there)

        self.plane(body)

    def finish(self):
        n = len(self.slots)
        await_rows(self.sum, 31 * n * 8, self.send.at[n + 1], self.recv.at[n + 1])


def sum_scratch(slots):
    return [pltpu.VMEM((n * slots, 128), F32) for n in (256, 8, 64)]


def main_kernel(
    scaling,     state_hbm, adjoint_hbm, gates_hbm, r0_ref, r1_ref, sum_ref, low_ref,
    state_ref, adjoint_ref, gates_ref, x_ref,
    y0, y1, z0, z1, w0, w1, one0, one1, one_new0, one_new1, two0, two1, two_new0, two_new1, part_ref,
    a1, a2, a3, b1, b2, b3,
    loads, sends, recvs, send_a, recv_a, send_b, recv_b,
):
    pairs = ((state_hbm, state_ref), (adjoint_hbm, adjoint_ref), (gates_hbm, gates_ref))
    copies = [pltpu.make_async_copy(src, dst, loads.at[i]) for i, (src, dst) in enumerate(pairs)]
    for copy in reversed(copies):
        copy.start()
    greet_all()
    fields = (state_ref, adjoint_ref)
    copies[2].wait()
    joined = join_low(gates_ref)
    copies[0].wait()
    copies[1].wait()
    undo_first(fields, gates_ref, x_ref)
    undo_low(joined, 0, x_ref, y0)
    early = GradientSum(part_ref, sum_ref, (0, 1), (a1, a2, a3), send_a, recv_a)
    late = GradientSum(part_ref, sum_ref, (2, 3, 4), (b1, b2, b3), send_b, recv_b)
    one = (one0, one_new0, two0, two_new0, w0)
    two = (one1, one_new1, two1, two_new1, w1)
    await_all()
    send_blocks(y0, z0, sends.at[0], recvs.at[0])
    first_gradients(fields, x_ref, part_ref)
    early.start_slot(0)
    early.start_slot(1)
    undo_low(joined, 1, x_ref, y1)
    send_blocks(y1, z1, sends.at[1], recvs.at[1])
    matrices = [undo_matrix(gates_ref, 2)] + [undo_lanes_matrix(gates_ref, k) for k in (4, 6)]
    early.start_columns()
    await_rows(z0, HALF - 4, sends.at[0], recvs.at[0])
    between_kernel(z0, *one, matrices)
    send_blocks(w0, r0_ref, sends.at[2], recvs.at[2])
    first = [gradient(k, *one) for k in range(3)]
    early.start_plane()
    await_rows(z1, HALF - 4, sends.at[1], recvs.at[1])

    def after(k):
        (re0, im0), (re1, im1) = first[k], gradient(k, *two)
        store_gradient(part_ref, 2 + k, re0 + re1, im0 + im1)
        late.start_slot(k)

    between_kernel(z1, *two, matrices, after)
    send_blocks(w1, r1_ref, sends.at[3], recvs.at[3], 0, 128)
    late.start_columns()
    send_blocks(w1, r1_ref, sends.at[3], recvs.at[3], 128, 256)
    early.finish()
    low_gradients(scaling, sum_ref, gates_ref, low_ref)
    late.start_plane()
    late.finish()
    for i, r_ref in enumerate((r0_ref, r1_ref)):
        await_rows(r_ref, HALF - 4, sends.at[2 + i], recvs.at[2 + i])


def finish_kernel(scaling, r0_ref, r1_ref, sum_ref, low_ref, state_ref, adjoint_ref, grads_ref):
    for m1, from_ref in enumerate((r0_ref, r1_ref)):
        for m0 in range(2):
            for v in range(4):
                rows = from_ref[pl.ds(m0 * 512 + v, 128, stride=4), :].T
                for r in range(2):
                    for f, ref in enumerate((state_ref, adjoint_ref)):
                        at = (r * 2 + f) * 32
                        ref[r, pl.ds(v * 4 + m1 * 2 + m0, 32, stride=16), :] = rows[at : at + 32]
    for k, slot in ((0, 0), (2, 2), (4, 3), (6, 4)):
        for r in range(2):
            grads_ref[k, r] = scaling * sum_ref[pl.ds(slot * 256 + r * 128, 128), :]
    for i in range(4):
        grads_ref[2 * i + 1] = low_ref[i]


VMEM = pl.BlockSpec(memory_space=pltpu.VMEM)


def local_call(kernel, outs, *args):
    return pl.pallas_call(
        kernel,
        out_shape=[jax.ShapeDtypeStruct(s, F32) for s in outs],
        in_specs=[VMEM] * len(args),
        out_specs=[VMEM] * len(outs),
        compiler_params=pltpu.CompilerParams(vmem_limit_bytes=48 << 20),
    )(*args)


def shards(state, adjoint, gates):
    scaling = float(N_DEV * 65536 // 128) ** -0.5
    half = pltpu.VMEM((HALF, 128), F32)
    hbm = pl.BlockSpec(memory_space=pltpu.HBM)
    inputs = (state.reshape(2, 512, 128), adjoint.reshape(2, 512, 128), gates)
    received = jax.ShapeDtypeStruct((HALF, 128), F32)
    r0, r1, sums, low = pl.pallas_call(
        functools.partial(main_kernel, scaling),
        out_shape=[
            received,
            received,
            jax.ShapeDtypeStruct((GROWS, 128), F32),
            jax.ShapeDtypeStruct((4, 2, 128, 128), F32),
        ],
        in_specs=[hbm] * 3,
        out_specs=[VMEM] * 4,
        scratch_shapes=[
            pltpu.VMEM((2, 512, 128), F32),
            pltpu.VMEM((2, 512, 128), F32),
            pltpu.VMEM((8, 2, 128, 128), F32),
            pltpu.VMEM((2048, 128), F32),
            *[half] * 14,
            pltpu.VMEM((GROWS, 128), F32),
            *sum_scratch(2),
            *sum_scratch(3),
            pltpu.SemaphoreType.DMA((3,)),
            pltpu.SemaphoreType.DMA((4,)),
            pltpu.SemaphoreType.DMA((4,)),
            *[pltpu.SemaphoreType.DMA((5,))] * 4,
        ],
        compiler_params=pltpu.CompilerParams(
            collective_id=0, has_side_effects=True, vmem_limit_bytes=40 << 20
        ),
    )(*(pltpu.with_memory_space_constraint(v, pltpu.HBM) for v in inputs))
    state_out, adjoint_out, grads_out = local_call(
        functools.partial(finish_kernel, scaling),
        [(2, 512, 128), (2, 512, 128), (8, 2, 128, 128)],
        r0, r1, sums, low,
    )
    return state_out.reshape(state.shape), adjoint_out.reshape(adjoint.shape), grads_out


def solution(mesh):
    in_specs = (P(None, "qa", "qb", None), P(None, "qa", "qb", None), P())
    out_specs = (P(None, "qa", "qb", None), P(None, "qa", "qb", None), P())
    return jax.shard_map(shards, mesh=mesh, in_specs=in_specs, out_specs=out_specs, check_vma=False)
```

```python
import functools

import jax
import jax.numpy as jnp
from jax import lax
from jax.experimental import pallas as pl
from jax.experimental.pallas import tpu as pltpu
from jax.sharding import PartitionSpec as P

F32 = jnp.float32
BF16 = jnp.bfloat16
MESH = pl.DeviceIdType.MESH
N_QA, N_QB, N_DEV = 8, 32, 256
HALF = N_DEV * 4
GROWS = 5 * 256


def split(x):
    hi = x.astype(BF16)
    return hi, (x - hi.astype(F32)).astype(BF16)


def dot3(a, b, ca, cb):
    ah, al = split(a)
    bh, bl = split(b)
    left = jnp.concatenate([ah, al, ah], axis=ca)
    right = jnp.concatenate([bh, bh, bl], axis=cb)
    return lax.dot_general(left, right, (((ca,), (cb,)), ((), ())), preferred_element_type=F32)


def conj_embed(re, im):
    return jnp.concatenate(
        [jnp.concatenate([re, -im], axis=1), jnp.concatenate([im, re], axis=1)], axis=0
    )


def undo_matrix(gates_ref, k):
    re, im = gates_ref[k, 0].T, gates_ref[k, 1].T
    hi, lo = split(
        jnp.concatenate(
            [jnp.concatenate([re, im], axis=1), jnp.concatenate([-im, re], axis=1)], axis=0
        )
    )
    return jnp.concatenate([hi, lo, hi], axis=1)


def undo_lanes_matrix(gates_ref, k):
    hi, lo = split(jnp.concatenate([gates_ref[k, 0].T, gates_ref[k, 1].T], axis=1))
    return jnp.concatenate([hi, lo, hi], axis=1)


def undo(matrix, x):
    hi, lo = split(x)
    return jnp.dot(matrix, jnp.concatenate([hi, hi, lo], axis=0), preferred_element_type=F32)


def quadrants(q):
    return q[:128, :128] + q[128:, 128:], q[128:, :128] - q[:128, 128:]


def cat(parts, axis):
    return jnp.concatenate(list(parts), axis=axis)


def store_gradient(part_ref, slot, re, im):
    part_ref[pl.ds(slot * 256, 128), :] = re
    part_ref[pl.ds(slot * 256 + 128, 128), :] = im


def undo_first(fields, gates_ref, x_ref):
    matrix = undo_matrix(gates_ref, 0)
    for f, ref in enumerate(fields):
        old = cat(
            (cat((ref[r, pl.ds(m, 128, stride=4), :] for m in range(4)), 1) for r in range(2)), 0
        )
        new = undo(matrix, old)
        for r in range(2):
            for m in range(4):
                x_ref[pl.ds(((f * 2 + r) * 4 + m) * 128, 128), :] = new[
                    r * 128 : (r + 1) * 128, m * 128 : (m + 1) * 128
                ]


def join_low(gates_ref):
    top = cat((gates_ref[1, 0], -gates_ref[1, 1]), 1)
    for k in (3, 5, 7):
        top = dot3(top, conj_embed(gates_ref[k, 0], gates_ref[k, 1]), 1, 0)
    return cat((top[:, :128].T, top[:, 128:].T), 1)


def undo_low(joined, m1, x_ref, y_ref):
    for m0 in range(2):
        straight, crossed = [], []
        for t21 in range(4):
            for f in range(2):
                for t0 in range(2):
                    re, im = (
                        x_ref[pl.ds(((f * 2 + r) * 4 + m1 * 2 + m0) * 128 + (t21 * 2 + t0) * 16, 16), :]
                        for r in range(2)
                    )
                    straight += [re, im]
                    crossed += [-im, re]
        out = dot3(joined, cat((cat(straight, 0), cat(crossed, 0)), 1), 1, 1)
        for t21 in range(4):
            y_ref[pl.ds(m0 * 512 + t21, 128, stride=4), :] = out[:, t21 * 128 : (t21 + 1) * 128]


def first_gradients(fields, x_ref, part_ref):
    old = cat(
        (cat((fields[1][r, pl.ds(m, 128, stride=4), :] for m in range(4)), 1) for r in range(2)), 0
    )
    new = cat((cat((x_ref[pl.ds((r * 4 + m) * 128, 128), :] for m in range(4)), 1) for r in range(2)), 0)
    store_gradient(part_ref, 0, *quadrants(dot3(old, new, 1, 1)))
    flat = [cat((ref[0], ref[1]), 1) for ref in fields]
    store_gradient(part_ref, 1, *quadrants(dot3(flat[1], flat[0], 0, 0)))


def turned(x):
    upper = lax.broadcasted_iota(jnp.int32, x.shape, 1) >= 64
    rolled = pltpu.roll(x, 64, 1)
    return jnp.where(upper, -rolled, rolled)


def load1(ref, f):
    return cat((ref[pl.ds((t0 * 2 + f) * 256, 256), :] for t0 in range(2)), 1)


def load2(ref, t):
    return ref[pl.ds(t * 128, 128), :]


def load3(ref, b1):
    return cat((ref[pl.ds(t * 128 + b1 * 16, 16), :] for t in range(8)), 0)


def undo_lanes(matrix, load):
    blocks = [load(i) for i in range(8)]
    return undo(matrix, cat((cat(blocks, 1), cat((turned(x) for x in blocks), 1)), 0))


def between_kernel(z_ref, one_ref, one_new_ref, two_ref, two_new_ref, w_ref, matrices, after=lambda k: None):
    for a in range(8):
        rows = cat((z_ref[pl.ds(a * 128 + t, 32, stride=4), :] for t in range(4)), 0).T
        for f in range(2):
            for t0 in range(2):
                for r in range(2):
                    at = ((f * 2 + t0) * 2 + r) * 16
                    one_ref[pl.ds((t0 * 2 + f) * 256 + r * 128 + a * 16, 16), :] = rows[at : at + 16]
    new = undo(matrices[0], cat((load1(one_ref, f) for f in range(2)), 1))
    for f in range(2):
        for t0 in range(2):
            one_new_ref[pl.ds((t0 * 2 + f) * 256, 256), :] = new[
                :, (f * 2 + t0) * 128 : (f * 2 + t0 + 1) * 128
            ]
    after(0)
    for t0 in range(2):
        for v in range(4):
            rows = cat(
                (
                    one_new_ref[pl.ds((t0 * 2 + f) * 256 + r * 128 + v, 32, stride=4), :]
                    for r in range(2)
                    for f in range(2)
                ),
                0,
            ).T
            for t in range(4):
                two_ref[pl.ds((t * 2 + t0) * 128 + v, 32, stride=4), :] = rows[t * 32 : (t + 1) * 32]
    new = undo_lanes(matrices[1], functools.partial(load2, two_ref))
    for t in range(8):
        two_new_ref[pl.ds(t * 128, 128), :] = new[:, t * 128 : (t + 1) * 128]
    after(1)
    new = undo_lanes(matrices[2], functools.partial(load3, two_new_ref))
    for b1 in range(8):
        w_ref[pl.ds(b1 * 128, 128), :] = new[:, b1 * 128 : (b1 + 1) * 128]
    after(2)


def lane_gradient(load_old, old_ref, load_new, new_ref):
    lane = lax.broadcasted_iota(jnp.int32, (128, 128), 1)
    adjoint = (lane & 32) != 0
    lefts, rights, crosses = [], [], []
    for i in range(0, 8, 2):
        lefts.append(
            jnp.where(adjoint, load_old(old_ref, i), pltpu.roll(load_old(old_ref, i + 1), 96, 1))
        )
        right = jnp.where(adjoint, pltpu.roll(load_new(new_ref, i), 32, 1), load_new(new_ref, i + 1))
        rights.append(right)
        crosses.append(-turned(right))
    q = dot3(cat(lefts, 1), cat((cat(rights, 1), cat(crosses, 1)), 0), 1, 1)
    return q[:, :128], q[:, 128:]


def gradient(k, one_ref, one_new_ref, two_ref, two_new_ref, w_ref):
    if k == 0:
        return quadrants(dot3(load1(one_ref, 1), load1(one_new_ref, 0), 1, 1))
    if k == 1:
        return lane_gradient(load2, two_ref, load2, two_new_ref)
    return lane_gradient(load3, two_new_ref, load2, w_ref)


def low_gradients(scaling, sum_ref, gates_ref, low_ref):
    rho = scaling * cat((sum_ref[pl.ds(256, 128), :], sum_ref[pl.ds(384, 128), :]), 1)
    for i, k in enumerate((1, 3, 5, 7)):
        re, im = gates_ref[k, 0], gates_ref[k, 1]
        grad = dot3(rho, conj_embed(re, -im), 1, 0)
        grad_re, grad_im = grad[:, :128], grad[:, 128:]
        low_ref[i, 0] = grad_re
        low_ref[i, 1] = grad_im
        if k < 7:
            right = cat((cat((grad_re, grad_im), 1), cat((grad_im, -grad_re), 1)), 0)
            rho = dot3(cat((re, im), 0), right, 0, 0)


def greet_all():
    qa, qb = lax.axis_index("qa"), lax.axis_index("qb")
    barrier = pltpu.get_barrier_semaphore()

    def greet(i, _):
        there = (lax.rem(qa + i // 32 + 4, 8), lax.rem(qb + lax.rem(i, 32) + 16, 32))
        pl.semaphore_signal(barrier, inc=1, device_id=there, device_id_type=MESH)
        return 0

    lax.fori_loop(0, 144, greet, 0)
    lax.fori_loop(145, N_DEV, greet, 0)


def await_all():
    pl.semaphore_wait(pltpu.get_barrier_semaphore(), N_DEV - 1)


def tile(index):
    return pl.ds(pl.multiple_of(index * 4, 4), 4)


def send_blocks(src_ref, dst_ref, send_sem, recv_sem, first=0, last=N_DEV):
    qa, qb = lax.axis_index("qa"), lax.axis_index("qb")
    me = qa * N_QB + qb

    def send(i, _):
        a, b = lax.rem(qa + i // 32, 8), lax.rem(qb + lax.rem(i, 32), 32)
        pltpu.make_async_remote_copy(
            src_ref=src_ref.at[tile(a * N_QB + b)],
            dst_ref=dst_ref.at[tile(me)],
            send_sem=send_sem,
            recv_sem=recv_sem,
            device_id=(a, b),
            device_id_type=MESH,
        ).start()
        return 0

    lax.fori_loop(max(first, 1), last, send, 0)
    if first == 0:
        dst_ref[tile(me), :] = src_ref[tile(me), :]


def await_rows(ref, rows, send_sem, recv_sem):
    qa, qb = lax.axis_index("qa"), lax.axis_index("qb")
    pltpu.make_async_remote_copy(
        src_ref=ref.at[pl.ds(0, rows)],
        dst_ref=ref.at[pl.ds(0, rows)],
        send_sem=send_sem,
        recv_sem=recv_sem,
        device_id=(qa, qb),
        device_id_type=MESH,
    ).wait()


def place():
    qa, qb = lax.axis_index("qa"), lax.axis_index("qb")
    return qb // 8, qa // 2, lax.rem(qa, 2) * 4 + lax.rem(qb // 2, 4), lax.rem(qb, 2)


def device(x, y, z, c):
    return (y * 2 + z // 4, x * 8 + lax.rem(z, 4) * 2 + c)


def rows_at(start, size):
    return pl.ds(pl.multiple_of(start, 8), size)


class GradientSum:
    def __init__(self, part_ref, sum_ref, slots, refs, send, recv):
        self.part, self.sum, self.slots = part_ref, sum_ref, slots
        self.got, self.mine, self.columns = refs
        self.send, self.recv = send, recv
        self.x, self.y, self.z, self.c = place()
        self.piece = self.y * 8 + self.x * 2 + self.c

    def put(self, stage, src, dst, there):
        pltpu.make_async_remote_copy(
            src_ref=src, dst_ref=dst, send_sem=self.send.at[stage], recv_sem=self.recv.at[stage],
            device_id=device(*there), device_id_type=MESH,
        ).start()

    def plane(self, body):
        def step(d, _):
            other = lax.rem(self.piece + d, 32)
            body(d, other, (lax.rem(other // 2, 4), other // 8, self.z, lax.rem(other, 2)))
            return 0

        lax.fori_loop(1, 32, step, 0)

    def rows(self, slot, piece):
        return rows_at(slot * 256 + piece * 8, 8)

    def start_slot(self, i):
        def body(d, other, there):
            self.put(i, self.part.at[self.rows(self.slots[i], other)], self.got.at[rows_at((i * 32 + d) * 8, 8)], there)

        self.plane(body)

    def start_columns(self):
        n = len(self.slots)
        for i, slot in enumerate(self.slots):
            await_rows(self.got, 31 * 8, self.send.at[i], self.recv.at[i])
            total = self.part[self.rows(slot, self.piece), :]
            for d in range(1, 32):
                total = total + self.got[(i * 32 + d) * 8 : (i * 32 + d + 1) * 8, :]
            self.mine[i * 8 : (i + 1) * 8, :] = total
        here = rows_at(self.z * n * 8, n * 8)
        for d in range(1, 8):
            self.put(n, self.mine, self.columns.at[here], (self.x, self.y, lax.rem(self.z + d, 8), self.c))
        self.columns[here, :] = self.mine[...]

    def start_plane(self):
        n = len(self.slots)
        await_rows(self.columns, 7 * n * 8, self.send.at[n], self.recv.at[n])
        for i, slot in enumerate(self.slots):
            total = self.columns[i * 8 : (i + 1) * 8, :]
            for k in range(1, 8):
                total = total + self.columns[(k * n + i) * 8 : (k * n + i + 1) * 8, :]
            self.sum[self.rows(slot, self.piece), :] = total

        def body(d, other, there):
            for slot in self.slots:
                mine = self.sum.at[self.rows(slot, self.piece)]
                self.put(n + 1, mine, mine, there)

        self.plane(body)

    def finish(self):
        n = len(self.slots)
        await_rows(self.sum, 31 * n * 8, self.send.at[n + 1], self.recv.at[n + 1])


def sum_scratch(slots):
    return [pltpu.VMEM((n * slots, 128), F32) for n in (256, 8, 64)]


def main_kernel(
    scaling,     state_hbm, adjoint_hbm, gates_hbm, r0_ref, r1_ref, sum_ref, low_ref,
    state_ref, adjoint_ref, gates_ref, x_ref,
    y0, y1, z0, z1, w0, w1, one0, one1, one_new0, one_new1, two0, two1, two_new0, two_new1, part_ref,
    a1, a2, a3, b1, b2, b3,
    loads, sends, recvs, send_a, recv_a, send_b, recv_b,
):
    pairs = ((state_hbm, state_ref), (adjoint_hbm, adjoint_ref), (gates_hbm, gates_ref))
    copies = [pltpu.make_async_copy(src, dst, loads.at[i]) for i, (src, dst) in enumerate(pairs)]
    for copy in reversed(copies):
        copy.start()
    greet_all()
    fields = (state_ref, adjoint_ref)
    copies[2].wait()
    joined = join_low(gates_ref)
    copies[0].wait()
    copies[1].wait()
    undo_first(fields, gates_ref, x_ref)
    undo_low(joined, 0, x_ref, y0)
    early = GradientSum(part_ref, sum_ref, (0, 1), (a1, a2, a3), send_a, recv_a)
    late = GradientSum(part_ref, sum_ref, (2, 3, 4), (b1, b2, b3), send_b, recv_b)
    one = (one0, one_new0, two0, two_new0, w0)
    two = (one1, one_new1, two1, two_new1, w1)
    await_all()
    send_blocks(y0, z0, sends.at[0], recvs.at[0])
    first_gradients(fields, x_ref, part_ref)
    early.start_slot(0)
    early.start_slot(1)
    undo_low(joined, 1, x_ref, y1)
    send_blocks(y1, z1, sends.at[1], recvs.at[1])
    matrices = [undo_matrix(gates_ref, 2)] + [undo_lanes_matrix(gates_ref, k) for k in (4, 6)]
    await_rows(z0, HALF - 4, sends.at[0], recvs.at[0])
    between_kernel(z0, *one, matrices)
    send_blocks(w0, r0_ref, sends.at[2], recvs.at[2])
    early.start_columns()
    first = [gradient(k, *one) for k in range(3)]
    await_rows(z1, HALF - 4, sends.at[1], recvs.at[1])

    def after(k):
        (re0, im0), (re1, im1) = first[k], gradient(k, *two)
        store_gradient(part_ref, 2 + k, re0 + re1, im0 + im1)
        late.start_slot(k)

    between_kernel(z1, *two, matrices, after)
    send_blocks(w1, r1_ref, sends.at[3], recvs.at[3], 0, 128)
    early.start_plane()
    late.start_columns()
    send_blocks(w1, r1_ref, sends.at[3], recvs.at[3], 128, 256)
    late.start_plane()
    early.finish()
    low_gradients(scaling, sum_ref, gates_ref, low_ref)
    late.finish()
    for i, r_ref in enumerate((r0_ref, r1_ref)):
        await_rows(r_ref, HALF - 4, sends.at[2 + i], recvs.at[2 + i])


def finish_kernel(scaling, r0_ref, r1_ref, sum_ref, low_ref, state_ref, adjoint_ref, grads_ref):
    for m1, from_ref in enumerate((r0_ref, r1_ref)):
        for m0 in range(2):
            for v in range(4):
                rows = from_ref[pl.ds(m0 * 512 + v, 128, stride=4), :].T
                for r in range(2):
                    for f, ref in enumerate((state_ref, adjoint_ref)):
                        at = (r * 2 + f) * 32
                        ref[r, pl.ds(v * 4 + m1 * 2 + m0, 32, stride=16), :] = rows[at : at + 32]
    for k, slot in ((0, 0), (2, 2), (4, 3), (6, 4)):
        for r in range(2):
            grads_ref[k, r] = scaling * sum_ref[pl.ds(slot * 256 + r * 128, 128), :]
    for i in range(4):
        grads_ref[2 * i + 1] = low_ref[i]


VMEM = pl.BlockSpec(memory_space=pltpu.VMEM)


def local_call(kernel, outs, *args):
    return pl.pallas_call(
        kernel,
        out_shape=[jax.ShapeDtypeStruct(s, F32) for s in outs],
        in_specs=[VMEM] * len(args),
        out_specs=[VMEM] * len(outs),
        compiler_params=pltpu.CompilerParams(vmem_limit_bytes=48 << 20),
    )(*args)


def shards(state, adjoint, gates):
    scaling = float(N_DEV * 65536 // 128) ** -0.5
    half = pltpu.VMEM((HALF, 128), F32)
    hbm = pl.BlockSpec(memory_space=pltpu.HBM)
    inputs = (state.reshape(2, 512, 128), adjoint.reshape(2, 512, 128), gates)
    received = jax.ShapeDtypeStruct((HALF, 128), F32)
    r0, r1, sums, low = pl.pallas_call(
        functools.partial(main_kernel, scaling),
        out_shape=[
            received,
            received,
            jax.ShapeDtypeStruct((GROWS, 128), F32),
            jax.ShapeDtypeStruct((4, 2, 128, 128), F32),
        ],
        in_specs=[hbm] * 3,
        out_specs=[VMEM] * 4,
        scratch_shapes=[
            pltpu.VMEM((2, 512, 128), F32),
            pltpu.VMEM((2, 512, 128), F32),
            pltpu.VMEM((8, 2, 128, 128), F32),
            pltpu.VMEM((2048, 128), F32),
            *[half] * 14,
            pltpu.VMEM((GROWS, 128), F32),
            *sum_scratch(2),
            *sum_scratch(3),
            pltpu.SemaphoreType.DMA((3,)),
            pltpu.SemaphoreType.DMA((4,)),
            pltpu.SemaphoreType.DMA((4,)),
            *[pltpu.SemaphoreType.DMA((5,))] * 4,
        ],
        compiler_params=pltpu.CompilerParams(
            collective_id=0, has_side_effects=True, vmem_limit_bytes=40 << 20
        ),
    )(*(pltpu.with_memory_space_constraint(v, pltpu.HBM) for v in inputs))
    state_out, adjoint_out, grads_out = local_call(
        functools.partial(finish_kernel, scaling),
        [(2, 512, 128), (2, 512, 128), (8, 2, 128, 128)],
        r0, r1, sums, low,
    )
    return state_out.reshape(state.shape), adjoint_out.reshape(adjoint.shape), grads_out


def solution(mesh):
    in_specs = (P(None, "qa", "qb", None), P(None, "qa", "qb", None), P())
    out_specs = (P(None, "qa", "qb", None), P(None, "qa", "qb", None), P())
    return jax.shard_map(shards, mesh=mesh, in_specs=in_specs, out_specs=out_specs, check_vma=False)
```

```python
import functools

import jax
import jax.numpy as jnp
from jax import lax
from jax.experimental import pallas as pl
from jax.experimental.pallas import tpu as pltpu
from jax.sharding import PartitionSpec as P

F32 = jnp.float32
BF16 = jnp.bfloat16
MESH = pl.DeviceIdType.MESH
N_QA, N_QB, N_DEV = 8, 32, 256
HALF = N_DEV * 4
GROWS = 5 * 256


def split(x):
    hi = x.astype(BF16)
    return hi, (x - hi.astype(F32)).astype(BF16)


def dot3(a, b, ca, cb):
    ah, al = split(a)
    bh, bl = split(b)
    left = jnp.concatenate([ah, al, ah], axis=ca)
    right = jnp.concatenate([bh, bh, bl], axis=cb)
    return lax.dot_general(left, right, (((ca,), (cb,)), ((), ())), preferred_element_type=F32)


def conj_embed(re, im):
    return jnp.concatenate(
        [jnp.concatenate([re, -im], axis=1), jnp.concatenate([im, re], axis=1)], axis=0
    )


def undo_matrix(gates_ref, k):
    re, im = gates_ref[k, 0].T, gates_ref[k, 1].T
    hi, lo = split(
        jnp.concatenate(
            [jnp.concatenate([re, im], axis=1), jnp.concatenate([-im, re], axis=1)], axis=0
        )
    )
    return jnp.concatenate([hi, lo, hi], axis=1)


def undo_lanes_matrix(gates_ref, k):
    hi, lo = split(jnp.concatenate([gates_ref[k, 0].T, gates_ref[k, 1].T], axis=1))
    return jnp.concatenate([hi, lo, hi], axis=1)


def undo(matrix, x):
    hi, lo = split(x)
    return jnp.dot(matrix, jnp.concatenate([hi, hi, lo], axis=0), preferred_element_type=F32)


def quadrants(q):
    return q[:128, :128] + q[128:, 128:], q[128:, :128] - q[:128, 128:]


def cat(parts, axis):
    return jnp.concatenate(list(parts), axis=axis)


def store_gradient(part_ref, slot, re, im):
    part_ref[pl.ds(slot * 256, 128), :] = re
    part_ref[pl.ds(slot * 256 + 128, 128), :] = im


def undo_first(fields, gates_ref, x_ref):
    matrix = undo_matrix(gates_ref, 0)
    for f, ref in enumerate(fields):
        old = cat(
            (cat((ref[r, pl.ds(m, 128, stride=4), :] for m in range(4)), 1) for r in range(2)), 0
        )
        new = undo(matrix, old)
        for r in range(2):
            for m in range(4):
                x_ref[pl.ds(((f * 2 + r) * 4 + m) * 128, 128), :] = new[
                    r * 128 : (r + 1) * 128, m * 128 : (m + 1) * 128
                ]


def join_low(gates_ref):
    top = cat((gates_ref[1, 0], -gates_ref[1, 1]), 1)
    for k in (3, 5, 7):
        top = dot3(top, conj_embed(gates_ref[k, 0], gates_ref[k, 1]), 1, 0)
    return cat((top[:, :128].T, top[:, 128:].T), 1)


def undo_low(joined, m1, x_ref, y_ref):
    for m0 in range(2):
        straight, crossed = [], []
        for t21 in range(4):
            for f in range(2):
                for t0 in range(2):
                    re, im = (
                        x_ref[pl.ds(((f * 2 + r) * 4 + m1 * 2 + m0) * 128 + (t21 * 2 + t0) * 16, 16), :]
                        for r in range(2)
                    )
                    straight += [re, im]
                    crossed += [-im, re]
        out = dot3(joined, cat((cat(straight, 0), cat(crossed, 0)), 1), 1, 1)
        for t21 in range(4):
            y_ref[pl.ds(m0 * 512 + t21, 128, stride=4), :] = out[:, t21 * 128 : (t21 + 1) * 128]


def first_gradients(fields, x_ref, part_ref):
    old = cat(
        (cat((fields[1][r, pl.ds(m, 128, stride=4), :] for m in range(4)), 1) for r in range(2)), 0
    )
    new = cat((cat((x_ref[pl.ds((r * 4 + m) * 128, 128), :] for m in range(4)), 1) for r in range(2)), 0)
    store_gradient(part_ref, 0, *quadrants(dot3(old, new, 1, 1)))
    flat = [cat((ref[0], ref[1]), 1) for ref in fields]
    store_gradient(part_ref, 1, *quadrants(dot3(flat[1], flat[0], 0, 0)))


def turned(x):
    upper = lax.broadcasted_iota(jnp.int32, x.shape, 1) >= 64
    rolled = pltpu.roll(x, 64, 1)
    return jnp.where(upper, -rolled, rolled)


def load1(ref, f):
    return cat((ref[pl.ds((t0 * 2 + f) * 256, 256), :] for t0 in range(2)), 1)


def load2(ref, t):
    return ref[pl.ds(t * 128, 128), :]


def load3(ref, b1):
    return cat((ref[pl.ds(t * 128 + b1 * 16, 16), :] for t in range(8)), 0)


def undo_lanes(matrix, load):
    blocks = [load(i) for i in range(8)]
    return undo(matrix, cat((cat(blocks, 1), cat((turned(x) for x in blocks), 1)), 0))


def between_kernel(z_ref, one_ref, one_new_ref, two_ref, two_new_ref, w_ref, matrices, after=lambda k: None):
    for a in range(8):
        rows = cat((z_ref[pl.ds(a * 128 + t, 32, stride=4), :] for t in range(4)), 0).T
        for f in range(2):
            for t0 in range(2):
                for r in range(2):
                    at = ((f * 2 + t0) * 2 + r) * 16
                    one_ref[pl.ds((t0 * 2 + f) * 256 + r * 128 + a * 16, 16), :] = rows[at : at + 16]
    new = undo(matrices[0], cat((load1(one_ref, f) for f in range(2)), 1))
    for f in range(2):
        for t0 in range(2):
            one_new_ref[pl.ds((t0 * 2 + f) * 256, 256), :] = new[
                :, (f * 2 + t0) * 128 : (f * 2 + t0 + 1) * 128
            ]
    after(0)
    for t0 in range(2):
        for v in range(4):
            rows = cat(
                (
                    one_new_ref[pl.ds((t0 * 2 + f) * 256 + r * 128 + v, 32, stride=4), :]
                    for r in range(2)
                    for f in range(2)
                ),
                0,
            ).T
            for t in range(4):
                two_ref[pl.ds((t * 2 + t0) * 128 + v, 32, stride=4), :] = rows[t * 32 : (t + 1) * 32]
    new = undo_lanes(matrices[1], functools.partial(load2, two_ref))
    for t in range(8):
        two_new_ref[pl.ds(t * 128, 128), :] = new[:, t * 128 : (t + 1) * 128]
    after(1)
    new = undo_lanes(matrices[2], functools.partial(load3, two_new_ref))
    for b1 in range(8):
        w_ref[pl.ds(b1 * 128, 128), :] = new[:, b1 * 128 : (b1 + 1) * 128]
    after(2)


def lane_gradient(load_old, old_ref, load_new, new_ref):
    lane = lax.broadcasted_iota(jnp.int32, (128, 128), 1)
    adjoint = (lane & 32) != 0
    lefts, rights, crosses = [], [], []
    for i in range(0, 8, 2):
        lefts.append(
            jnp.where(adjoint, load_old(old_ref, i), pltpu.roll(load_old(old_ref, i + 1), 96, 1))
        )
        right = jnp.where(adjoint, pltpu.roll(load_new(new_ref, i), 32, 1), load_new(new_ref, i + 1))
        rights.append(right)
        crosses.append(-turned(right))
    q = dot3(cat(lefts, 1), cat((cat(rights, 1), cat(crosses, 1)), 0), 1, 1)
    return q[:, :128], q[:, 128:]


def gradient(k, one_ref, one_new_ref, two_ref, two_new_ref, w_ref):
    if k == 0:
        return quadrants(dot3(load1(one_ref, 1), load1(one_new_ref, 0), 1, 1))
    if k == 1:
        return lane_gradient(load2, two_ref, load2, two_new_ref)
    return lane_gradient(load3, two_new_ref, load2, w_ref)


def low_gradients(scaling, sum_ref, gates_ref, low_ref):
    rho = scaling * cat((sum_ref[pl.ds(256, 128), :], sum_ref[pl.ds(384, 128), :]), 1)
    for i, k in enumerate((1, 3, 5, 7)):
        re, im = gates_ref[k, 0], gates_ref[k, 1]
        grad = dot3(rho, conj_embed(re, -im), 1, 0)
        grad_re, grad_im = grad[:, :128], grad[:, 128:]
        low_ref[i, 0] = grad_re
        low_ref[i, 1] = grad_im
        if k < 7:
            right = cat((cat((grad_re, grad_im), 1), cat((grad_im, -grad_re), 1)), 0)
            rho = dot3(cat((re, im), 0), right, 0, 0)


def greet_all():
    qa, qb = lax.axis_index("qa"), lax.axis_index("qb")
    barrier = pltpu.get_barrier_semaphore()

    def greet(i, _):
        there = (lax.rem(qa + i // 32 + 4, 8), lax.rem(qb + lax.rem(i, 32) + 16, 32))
        pl.semaphore_signal(barrier, inc=1, device_id=there, device_id_type=MESH)
        return 0

    lax.fori_loop(0, 144, greet, 0)
    lax.fori_loop(145, N_DEV, greet, 0)


def await_all():
    pl.semaphore_wait(pltpu.get_barrier_semaphore(), N_DEV - 1)


def tile(index):
    return pl.ds(pl.multiple_of(index * 4, 4), 4)


def send_blocks(src_ref, dst_ref, send_sem, recv_sem, first=0, last=N_DEV):
    qa, qb = lax.axis_index("qa"), lax.axis_index("qb")
    me = qa * N_QB + qb

    def send(i, _):
        a, b = lax.rem(qa + i // 32, 8), lax.rem(qb + lax.rem(i, 32), 32)
        pltpu.make_async_remote_copy(
            src_ref=src_ref.at[tile(a * N_QB + b)],
            dst_ref=dst_ref.at[tile(me)],
            send_sem=send_sem,
            recv_sem=recv_sem,
            device_id=(a, b),
            device_id_type=MESH,
        ).start()
        return 0

    lax.fori_loop(max(first, 1), last, send, 0)
    if first == 0:
        dst_ref[tile(me), :] = src_ref[tile(me), :]


def await_rows(ref, rows, send_sem, recv_sem):
    qa, qb = lax.axis_index("qa"), lax.axis_index("qb")
    pltpu.make_async_remote_copy(
        src_ref=ref.at[pl.ds(0, rows)],
        dst_ref=ref.at[pl.ds(0, rows)],
        send_sem=send_sem,
        recv_sem=recv_sem,
        device_id=(qa, qb),
        device_id_type=MESH,
    ).wait()


def place():
    qa, qb = lax.axis_index("qa"), lax.axis_index("qb")
    return qb // 8, qa // 2, lax.rem(qa, 2) * 4 + lax.rem(qb // 2, 4), lax.rem(qb, 2)


def device(x, y, z, c):
    return (y * 2 + z // 4, x * 8 + lax.rem(z, 4) * 2 + c)


def rows_at(start, size):
    return pl.ds(pl.multiple_of(start, 8), size)


class GradientSum:
    def __init__(self, part_ref, sum_ref, slots, refs, send, recv):
        self.part, self.sum, self.slots = part_ref, sum_ref, slots
        self.got, self.mine, self.columns = refs
        self.send, self.recv = send, recv
        self.x, self.y, self.z, self.c = place()
        self.piece = self.y * 8 + self.x * 2 + self.c

    def put(self, stage, src, dst, there):
        pltpu.make_async_remote_copy(
            src_ref=src, dst_ref=dst, send_sem=self.send.at[stage], recv_sem=self.recv.at[stage],
            device_id=device(*there), device_id_type=MESH,
        ).start()

    def plane(self, body):
        def step(d, _):
            other = lax.rem(self.piece + d, 32)
            body(d, other, (lax.rem(other // 2, 4), other // 8, self.z, lax.rem(other, 2)))
            return 0

        lax.fori_loop(1, 32, step, 0)

    def rows(self, slot, piece):
        return rows_at(slot * 256 + piece * 8, 8)

    def start_slot(self, i):
        def body(d, other, there):
            self.put(i, self.part.at[self.rows(self.slots[i], other)], self.got.at[rows_at((i * 32 + d) * 8, 8)], there)

        self.plane(body)

    def start_columns(self):
        n = len(self.slots)
        for i, slot in enumerate(self.slots):
            await_rows(self.got, 31 * 8, self.send.at[i], self.recv.at[i])
            total = self.part[self.rows(slot, self.piece), :]
            for d in range(1, 32):
                total = total + self.got[(i * 32 + d) * 8 : (i * 32 + d + 1) * 8, :]
            self.mine[i * 8 : (i + 1) * 8, :] = total
        here = rows_at(self.z * n * 8, n * 8)
        for d in range(1, 8):
            self.put(n, self.mine, self.columns.at[here], (self.x, self.y, lax.rem(self.z + d, 8), self.c))
        self.columns[here, :] = self.mine[...]

    def start_plane(self):
        n = len(self.slots)
        await_rows(self.columns, 7 * n * 8, self.send.at[n], self.recv.at[n])
        for i, slot in enumerate(self.slots):
            total = self.columns[i * 8 : (i + 1) * 8, :]
            for k in range(1, 8):
                total = total + self.columns[(k * n + i) * 8 : (k * n + i + 1) * 8, :]
            self.sum[self.rows(slot, self.piece), :] = total

        def body(d, other, there):
            for slot in self.slots:
                mine = self.sum.at[self.rows(slot, self.piece)]
                self.put(n + 1, mine, mine, there)

        self.plane(body)

    def finish(self):
        n = len(self.slots)
        await_rows(self.sum, 31 * n * 8, self.send.at[n + 1], self.recv.at[n + 1])


def sum_scratch(slots):
    return [pltpu.VMEM((n * slots, 128), F32) for n in (256, 8, 64)]


def main_kernel(
    scaling,     state_hbm, adjoint_hbm, gates_hbm, r0_ref, r1_ref, sum_ref, low_ref,
    state_ref, adjoint_ref, gates_ref, x_ref,
    y0, y1, z0, z1, w0, w1, one0, one1, one_new0, one_new1, two0, two1, two_new0, two_new1, part_ref,
    a1, a2, a3, b1, b2, b3,
    loads, sends, recvs, send_a, recv_a, send_b, recv_b,
):
    pairs = ((state_hbm, state_ref), (adjoint_hbm, adjoint_ref), (gates_hbm, gates_ref))
    copies = [pltpu.make_async_copy(src, dst, loads.at[i]) for i, (src, dst) in enumerate(pairs)]
    for copy in reversed(copies):
        copy.start()
    greet_all()
    fields = (state_ref, adjoint_ref)
    copies[2].wait()
    joined = join_low(gates_ref)
    copies[0].wait()
    copies[1].wait()
    undo_first(fields, gates_ref, x_ref)
    undo_low(joined, 0, x_ref, y0)
    early = GradientSum(part_ref, sum_ref, (0, 1), (a1, a2, a3), send_a, recv_a)
    late = GradientSum(part_ref, sum_ref, (2, 3, 4), (b1, b2, b3), send_b, recv_b)
    one = (one0, one_new0, two0, two_new0, w0)
    two = (one1, one_new1, two1, two_new1, w1)
    await_all()
    send_blocks(y0, z0, sends.at[0], recvs.at[0])
    first_gradients(fields, x_ref, part_ref)
    early.start_slot(0)
    early.start_slot(1)
    undo_low(joined, 1, x_ref, y1)
    send_blocks(y1, z1, sends.at[1], recvs.at[1])
    matrices = [undo_matrix(gates_ref, 2)] + [undo_lanes_matrix(gates_ref, k) for k in (4, 6)]
    await_rows(z0, HALF - 4, sends.at[0], recvs.at[0])
    between_kernel(z0, *one, matrices)
    send_blocks(w0, r0_ref, sends.at[2], recvs.at[2])
    early.start_columns()
    first = [gradient(k, *one) for k in range(3)]
    await_rows(z1, HALF - 4, sends.at[1], recvs.at[1])

    def after(k):
        (re0, im0), (re1, im1) = first[k], gradient(k, *two)
        store_gradient(part_ref, 2 + k, re0 + re1, im0 + im1)
        late.start_slot(k)

    between_kernel(z1, *two, matrices, after)
    send_blocks(w1, r1_ref, sends.at[3], recvs.at[3], 0, 128)
    late.start_columns()
    send_blocks(w1, r1_ref, sends.at[3], recvs.at[3], 128, 256)
    early.start_plane()
    late.start_plane()
    early.finish()
    low_gradients(scaling, sum_ref, gates_ref, low_ref)
    late.finish()
    for i, r_ref in enumerate((r0_ref, r1_ref)):
        await_rows(r_ref, HALF - 4, sends.at[2 + i], recvs.at[2 + i])


def finish_kernel(scaling, r0_ref, r1_ref, sum_ref, low_ref, state_ref, adjoint_ref, grads_ref):
    for m1, from_ref in enumerate((r0_ref, r1_ref)):
        for m0 in range(2):
            for v in range(4):
                rows = from_ref[pl.ds(m0 * 512 + v, 128, stride=4), :].T
                for r in range(2):
                    for f, ref in enumerate((state_ref, adjoint_ref)):
                        at = (r * 2 + f) * 32
                        ref[r, pl.ds(v * 4 + m1 * 2 + m0, 32, stride=16), :] = rows[at : at + 32]
    for k, slot in ((0, 0), (2, 2), (4, 3), (6, 4)):
        for r in range(2):
            grads_ref[k, r] = scaling * sum_ref[pl.ds(slot * 256 + r * 128, 128), :]
    for i in range(4):
        grads_ref[2 * i + 1] = low_ref[i]


VMEM = pl.BlockSpec(memory_space=pltpu.VMEM)


def local_call(kernel, outs, *args):
    return pl.pallas_call(
        kernel,
        out_shape=[jax.ShapeDtypeStruct(s, F32) for s in outs],
        in_specs=[VMEM] * len(args),
        out_specs=[VMEM] * len(outs),
        compiler_params=pltpu.CompilerParams(vmem_limit_bytes=48 << 20),
    )(*args)


def shards(state, adjoint, gates):
    scaling = float(N_DEV * 65536 // 128) ** -0.5
    half = pltpu.VMEM((HALF, 128), F32)
    hbm = pl.BlockSpec(memory_space=pltpu.HBM)
    inputs = (state.reshape(2, 512, 128), adjoint.reshape(2, 512, 128), gates)
    received = jax.ShapeDtypeStruct((HALF, 128), F32)
    r0, r1, sums, low = pl.pallas_call(
        functools.partial(main_kernel, scaling),
        out_shape=[
            received,
            received,
            jax.ShapeDtypeStruct((GROWS, 128), F32),
            jax.ShapeDtypeStruct((4, 2, 128, 128), F32),
        ],
        in_specs=[hbm] * 3,
        out_specs=[VMEM] * 4,
        scratch_shapes=[
            pltpu.VMEM((2, 512, 128), F32),
            pltpu.VMEM((2, 512, 128), F32),
            pltpu.VMEM((8, 2, 128, 128), F32),
            pltpu.VMEM((2048, 128), F32),
            *[half] * 14,
            pltpu.VMEM((GROWS, 128), F32),
            *sum_scratch(2),
            *sum_scratch(3),
            pltpu.SemaphoreType.DMA((3,)),
            pltpu.SemaphoreType.DMA((4,)),
            pltpu.SemaphoreType.DMA((4,)),
            *[pltpu.SemaphoreType.DMA((5,))] * 4,
        ],
        compiler_params=pltpu.CompilerParams(
            collective_id=0, has_side_effects=True, vmem_limit_bytes=40 << 20
        ),
    )(*(pltpu.with_memory_space_constraint(v, pltpu.HBM) for v in inputs))
    state_out, adjoint_out, grads_out = local_call(
        functools.partial(finish_kernel, scaling),
        [(2, 512, 128), (2, 512, 128), (8, 2, 128, 128)],
        r0, r1, sums, low,
    )
    return state_out.reshape(state.shape), adjoint_out.reshape(adjoint.shape), grads_out


def solution(mesh):
    in_specs = (P(None, "qa", "qb", None), P(None, "qa", "qb", None), P())
    out_specs = (P(None, "qa", "qb", None), P(None, "qa", "qb", None), P())
    return jax.shard_map(shards, mesh=mesh, in_specs=in_specs, out_specs=out_specs, check_vma=False)
```
